32 devices in a mesh: sec: 8 (over y, x, core), strip: 4 (over z).
Axes of the slice: x: 2, y: 2, z: 4, core: 2. Of those that a mesh axis runs over, the one named last changes fastest.
Arguments:
- start_offsets: float32 [2, 8, 384, 2048], P(None, 'sec', 'strip'), may hold values from -0.4 to 0.4
- section_flow: float32 [2, 8, 384, 2048], P(None, 'sec', 'strip'), may hold values from -1.5 to 1.5, as said below
- fixed_nodes: int32 [8, 384, 2048], P('sec', 'strip'), may hold values 0 or 1
- links_across: int32 [8, 384, 2048], P('sec', 'strip'), may hold values 0 or 1
- links_down: int32 [8, 384, 2048], P('sec', 'strip'), may hold values 0 or 1
Outputs:
- final_offsets: float32 [2, 8, 384, 2048], P(None, 'sec', 'strip')
- final_speeds: float32 [2, 8, 384, 2048], P(None, 'sec', 'strip')
The draws below stay inside these ranges and needn't reach their ends.
Inputs may be any that keep to these rules, and one draw needn't show every extreme that they name: `section_flow`: entries of section 0 take part in no spring.
All inputs are finite; a program needn't handle non-finite values. No bound on the sum of `fixed_nodes` or of `links_across` or of `links_down` on one device may be relied on, other than what follows from the above.
Results may differ from the reference program's by a relative error of at most 0.00017.
Values sent between devices are 32-bit elements; how exact they have to be, the bound alone decides.
No kernel may reach another device: no remote copies, remote signals or barrier semaphores. Data moves between devices by JAX's collectives and lax.ppermute only.
A program may use at most 64 MiB of HBM per device.

```python
import jax
import jax.numpy as jnp
from jax import lax

COLS = 2048
SWEEPS = 2
ROUNDS = 2
SUBSTEPS = 4
SECTIONS = 8
ROWS = 384


def draw_section_flow(key, part):
    subkeys = jax.random.split(key, 1)
    section_index = jnp.arange(SECTIONS).astype(jnp.float32)
    section_ramp = 0.12 * (0.5 + section_index / max(SECTIONS - 1, 1))
    normal_part = jax.random.truncated_normal(subkeys[0], -4.0, 4.0, (2, SECTIONS, ROWS, COLS), jnp.float32)
    sample = normal_part * section_ramp[None, :, None, None]
    return sample.astype(jnp.float32)


def place_ends(result, rng, low, high):
    extent = result.shape
    place = [jax.random.randint(jax.random.fold_in(rng, axis), (), 0, extent[axis]) for axis in range(len(extent))]
    result = result.at[tuple(place)].set(low)
    longest = extent.index(max(extent))
    place[longest] = (place[longest] + 1) % extent[longest]
    return result.at[tuple(place)].set(high)


def shard_levels(stream_key, shape, cuts, least, high):
    def one(axis_at, shards_of):
        steps = jax.random.uniform(jax.random.fold_in(jax.random.fold_in(stream_key, 6), axis_at), (shards_of,), jnp.float32, least / len(cuts), high / len(cuts))
        return jnp.repeat(jnp.exp(steps), shape[axis_at] // shards_of).reshape((-1,) + (1,) * (len(shape) - axis_at - 1))

    loudness = one(*cuts[0])
    for cut in cuts[1:]:
        loudness = loudness * one(*cut)
    return loudness


def centred(stream_key, dims, width, bound, cuts=(), kind=jnp.bfloat16):
    gain = shard_levels(stream_key, dims, cuts, -0.22, 0.18) if cuts else 1.0
    result = jax.random.normal(stream_key, dims, jnp.float32) * width * gain
    return jnp.minimum(jnp.maximum(result, -bound), bound).astype(kind)


def setup_inputs(seed: int = 0) -> dict:
    splits = jax.random.split(jax.random.key(seed), 6)
    return {
        "start_offsets": centred(splits[0], (2, SECTIONS, ROWS, COLS), 0.08, 0.4, ((1, 8), (2, 4)), jnp.float32),
        "section_flow": draw_section_flow(jax.random.fold_in(splits[5], 71), 0),
        "fixed_nodes": place_ends((jax.random.randint(splits[2], (SECTIONS, ROWS, COLS), 0, 16) < 1).astype(jnp.int32), jax.random.fold_in(splits[2], 1), 0, 1),
        "links_across": place_ends((jax.random.randint(splits[3], (SECTIONS, ROWS, COLS), 0, 16) < 15).astype(jnp.int32), jax.random.fold_in(splits[3], 1), 0, 1),
        "links_down": place_ends((jax.random.randint(splits[4], (SECTIONS, ROWS, COLS), 0, 16) < 15).astype(jnp.int32), jax.random.fold_in(splits[4], 1), 0, 1),
    }


SPRING = 1.0
COUPLING = 0.5
STEP_SIZE = 0.4
DAMPING = 0.9
SPEED_CAP = 0.05
EPSILON = 1e-06

def along_cols(values, lower, upper):
    widths = [(0, 0)] * (values.ndim - 1) + [(lower, upper)]
    return jnp.pad(values, widths)

def along_rows(values, lower, upper):
    widths = [(0, 0)] * (values.ndim - 2) + [(lower, upper), (0, 0)]
    return jnp.pad(values, widths)

def spring_forces(offsets, across, down):
    across_x = offsets[0, ..., 1:] - offsets[0, ..., :-1] + 1.0
    across_y = offsets[1, ..., 1:] - offsets[1, ..., :-1]
    tension = 0.5 * SPRING * (across_x * across_x + across_y * across_y - 1.0) * across[..., :-1]
    force_x = along_cols(tension * across_x, 0, 1) - along_cols(tension * across_x, 1, 0)
    force_y = along_cols(tension * across_y, 0, 1) - along_cols(tension * across_y, 1, 0)
    down_x = offsets[0, ..., 1:, :] - offsets[0, ..., :-1, :]
    down_y = offsets[1, ..., 1:, :] - offsets[1, ..., :-1, :] + 1.0
    strain = 0.5 * SPRING * (down_x * down_x + down_y * down_y - 1.0) * down[..., :-1, :]
    force_x = force_x + along_rows(strain * down_x, 0, 1) - along_rows(strain * down_x, 1, 0)
    force_y = force_y + along_rows(strain * down_y, 0, 1) - along_rows(strain * down_y, 1, 0)
    return jnp.stack([force_x, force_y])

def advance(offsets, speeds, across, down, mobility, target, section_links):
    force = spring_forces(offsets, across, down) + COUPLING * (target - section_links * offsets)
    speeds = mobility * (DAMPING * speeds + STEP_SIZE * force)
    return (offsets + STEP_SIZE * speeds, speeds)

def reference(start_offsets, section_flow, fixed_nodes, links_across, links_down):
    column_index = jnp.arange(COLS)
    row_index = jnp.arange(ROWS)
    across = links_across.astype(jnp.float32) * (column_index < COLS - 1).astype(jnp.float32)
    down = links_down.astype(jnp.float32) * (row_index < ROWS - 1).astype(jnp.float32)[:, None]
    mobility = 1.0 - fixed_nodes.astype(jnp.float32)
    section_index = jnp.arange(SECTIONS)
    has_below = (section_index > 0).astype(jnp.float32)
    has_above = (section_index < SECTIONS - 1).astype(jnp.float32)
    section_links = has_below + has_above
    offsets = start_offsets
    speeds = jnp.zeros_like(start_offsets)
    empty = jnp.zeros_like(start_offsets[:, :1])

    def relax(section_item):
        here_offsets, here_speeds, here_across, here_down, here_mobility, here_target, here_links = section_item
        for substep_id in range(SUBSTEPS):
            here_offsets, here_speeds = advance(here_offsets, here_speeds, here_across, here_down, here_mobility, here_target, here_links)
        return (here_offsets, here_speeds)
    for sweep_id in range(SWEEPS):
        below = jnp.concatenate([empty, offsets[:, :-1]], axis=1) + section_flow
        above = jnp.concatenate([offsets[:, 1:] - section_flow[:, 1:], empty], axis=1)
        target = has_below[:, None, None] * below + has_above[:, None, None] * above
        for round_id in range(ROUNDS):
            power = jnp.sum(speeds * speeds)
            spread = jnp.sqrt(power / (2.0 * SECTIONS * ROWS * COLS) + EPSILON)
            speeds = speeds * jnp.minimum(1.0, SPEED_CAP / spread)
            moved = lax.map(relax, (jnp.moveaxis(offsets, 1, 0), jnp.moveaxis(speeds, 1, 0), across, down, mobility, jnp.moveaxis(target, 1, 0), section_links))
            offsets = jnp.moveaxis(moved[0], 0, 1)
            speeds = jnp.moveaxis(moved[1], 0, 1)
    return (offsets, speeds)
```

```python
import functools

import jax
import jax.numpy as jnp
from jax import lax
from jax.experimental import pallas as pl
from jax.experimental.pallas import tpu as pltpu
from jax.sharding import PartitionSpec as P

SWEEPS = 2
ROUNDS = 2
SUBSTEPS = 4

SPRING = 1.0
COUPLING = 0.5
STEP_SIZE = 0.4
DAMPING = 0.9
SPEED_CAP = 0.05
EPSILON = 1e-06

LANES = 128
SUBLANES = 8
HALO = 8
SPRING_WEIGHT = 0.5 * SPRING * STEP_SIZE * STEP_SIZE
PULL_WEIGHT = COUPLING * STEP_SIZE * STEP_SIZE


def round_kernel(first, last, entries, pull_ref, part_ref, u_ref, v_ref, t_ref, w_ref, uo_ref, vo_ref, po_ref, s1, s2, g):
    tiles, cols = (u_ref.shape[1], u_ref.shape[3] // LANES)
    shape = (SUBLANES, LANES)
    lane = lax.broadcasted_iota(jnp.int32, shape, 1)
    sub = lax.broadcasted_iota(jnp.int32, shape, 0)
    lane_first, lane_last = (lane == 0, lane == LANES - 1)
    sub_first, sub_last = (sub == 0, sub == SUBLANES - 1)
    pull = jnp.full(shape, pull_ref[0], jnp.float32)
    if first:
        damp0 = None
    else:
        power = jnp.sum(part_ref[...]) / (STEP_SIZE * STEP_SIZE)
        spread = jnp.sqrt(jnp.full(shape, power / entries + EPSILON, jnp.float32))
        damp0 = DAMPING * jnp.minimum(1.0, SPEED_CAP / spread)
    out_scale = 1.0 / STEP_SIZE

    def substep(step, src, dst):
        vsrc = v_ref if step == 0 else vo_ref
        final = step == SUBSTEPS - 1
        zero = jnp.zeros(shape, jnp.float32)
        for c in range(cols):
            cs = slice(c * LANES, (c + 1) * LANES)
            g[0, :, cs] = zero
            g[1, :, cs] = zero

        def row(r, acc):
            below = jnp.minimum(r + 1, tiles - 1)
            load = lambda ref, i, t, c: ref[i, t, :, c * LANES:(c + 1) * LANES]
            ux, uy = (load(src, 0, r, 0), load(src, 1, r, 0))
            ux0, uy0 = (ux, uy)
            fx_prev, fy_prev = (zero, zero)
            for c in range(cols):
                cs = slice(c * LANES, (c + 1) * LANES)
                if c + 1 < cols:
                    nx, ny = (load(src, 0, r, c + 1), load(src, 1, r, c + 1))
                else:
                    nx, ny = (ux0, uy0)
                ax = pltpu.roll(jnp.where(lane_first, nx, ux), LANES - 1, 1) - ux
                ay = pltpu.roll(jnp.where(lane_first, ny, uy), LANES - 1, 1) - uy
                ex = ax + 1.0
                t = (ex * ex + ay * ay - 1.0) * load(w_ref, 0, r, c)
                fx, fy = (t * ex, t * ay)
                px = pltpu.roll(jnp.where(lane_last, fx_prev, fx), 1, 1)
                py = pltpu.roll(jnp.where(lane_last, fy_prev, fy), 1, 1)
                bx, by = (load(src, 0, below, c), load(src, 1, below, c))
                dx = pltpu.roll(jnp.where(sub_first, bx, ux), SUBLANES - 1, 0) - ux
                dy = pltpu.roll(jnp.where(sub_first, by, uy), SUBLANES - 1, 0) - uy
                ey = dy + 1.0
                q = (dx * dx + ey * ey - 1.0) * load(w_ref, 1, r, c)
                gx, gy = (q * dx, q * ey)
                hx = pltpu.roll(jnp.where(sub_last, g[0, :, cs], gx), 1, 0)
                hy = pltpu.roll(jnp.where(sub_last, g[1, :, cs], gy), 1, 0)
                g[0, :, cs] = gx
                g[1, :, cs] = gy
                ax = (fx - px) + (gx - hx) + (load(t_ref, 0, r, c) - pull * ux)
                ay = (fy - py) + (gy - hy) + (load(t_ref, 1, r, c) - pull * uy)
                if not (first and step == 0):
                    damp = damp0 if step == 0 else DAMPING
                    ax = ax + damp * load(vsrc, 0, r, c)
                    ay = ay + damp * load(vsrc, 1, r, c)
                m = load(w_ref, 2, r, c)
                vx, vy = (m * ax, m * ay)
                dst[0, r, :, cs] = ux + vx
                dst[1, r, :, cs] = uy + vy
                if final and last:
                    vo_ref[0, r, :, cs] = vx * out_scale
                    vo_ref[1, r, :, cs] = vy * out_scale
                else:
                    vo_ref[0, r, :, cs] = vx
                    vo_ref[1, r, :, cs] = vy
                if final and not last:
                    acc = acc + (vx * vx + vy * vy)
                ux, uy, fx_prev, fy_prev = (nx, ny, fx, fy)
            return acc

        if final and not last:
            head = HALO // SUBLANES
            row(0, zero)
            acc = lax.fori_loop(head, tiles - head, row, zero)
            row(tiles - 1, zero)
            po_ref[...] = jnp.broadcast_to(jnp.sum(acc, 0, keepdims=True)[None], po_ref.shape)
        else:
            lax.fori_loop(0, tiles, row, jnp.zeros(shape, jnp.float32))

    substep(0, u_ref, s1)
    substep(1, s1, s2)
    substep(2, s2, s1)
    substep(3, s1, uo_ref)


def run_round(first, last, entries, devices, pull, part, u, v, t, w):
    vm = pl.BlockSpec(memory_space=pltpu.VMEM)
    return pl.pallas_call(
        functools.partial(round_kernel, first, last, entries),
        out_shape=(
            jax.ShapeDtypeStruct(u.shape, jnp.float32),
            jax.ShapeDtypeStruct(u.shape, jnp.float32),
            jax.ShapeDtypeStruct((devices, 1, LANES), jnp.float32),
        ),
        in_specs=[pl.BlockSpec(memory_space=pltpu.SMEM)] + [vm] * 5 + [vm][:0],
        out_specs=(vm, vm, vm),
        scratch_shapes=[
            pltpu.VMEM(u.shape, jnp.float32),
            pltpu.VMEM(u.shape, jnp.float32),
            pltpu.VMEM((2, SUBLANES, u.shape[3]), jnp.float32),
        ],
        compiler_params=pltpu.CompilerParams(vmem_limit_bytes=24 << 20),
    )(pull, part, u, v, t, w)


def extended(x, dim, width):
    peers, length = (lax.axis_size("strip"), x.shape[dim])
    up = [(i, (i + 1) % peers) for i in range(peers - 1)]
    down = [(j, i) for i, j in up]
    before = lax.ppermute(lax.slice_in_dim(x, length - width, length, axis=dim), "strip", up)
    after = lax.ppermute(lax.slice_in_dim(x, 0, width, axis=dim), "strip", down)
    return jnp.concatenate([before, x, after], axis=dim)


def tiled(x):
    return x.reshape(x.shape[0], x.shape[1] // SUBLANES, SUBLANES, x.shape[2])


def untiled(x):
    return x.reshape(x.shape[0], x.shape[1] * SUBLANES, x.shape[3])


def on_device(start_offsets, section_flow, fixed_nodes, links_across, links_down):
    axes = ("sec", "strip")
    sections, strips = (lax.axis_size("sec"), lax.axis_size("strip"))
    devices = sections * strips
    _, rows, columns = fixed_nodes.shape
    total_rows = rows * strips
    entries = 2.0 * sections * total_rows * columns
    s = lax.axis_index("sec")
    has_below = (s > 0).astype(jnp.float32)
    has_above = (s < sections - 1).astype(jnp.float32)
    pull = (PULL_WEIGHT * (has_below + has_above)).reshape(1)
    column_index = jnp.arange(columns)
    row_index = lax.axis_index("strip") * rows + jnp.arange(rows)
    across = jnp.where(column_index < columns - 1, links_across[0].astype(jnp.float32) * SPRING_WEIGHT, 0.0)
    down = jnp.where((row_index < total_rows - 1)[:, None], links_down[0].astype(jnp.float32) * SPRING_WEIGHT, 0.0)
    mobility = 1.0 - fixed_nodes[0].astype(jnp.float32)
    w = tiled(extended(jnp.stack([across, down, mobility]), 1, HALO))
    u, v = (start_offsets[:, 0], None)
    flow = section_flow[:, 0]
    up = [(i, i + 1) for i in range(sections - 1)]
    dn = [(j, i) for i, j in up]
    part = jnp.zeros((devices, 1, LANES), jnp.float32)
    for sweep in range(SWEEPS):
        lower = lax.ppermute(u, "sec", up)
        upper = lax.ppermute(u - flow, "sec", dn)
        t = PULL_WEIGHT * (has_below * (lower + flow) + has_above * upper)
        if sweep == 0:
            state = extended(jnp.concatenate([u, t]), 1, HALO)
            ux, tx, vx = (tiled(state[:2]), tiled(state[2:]), tiled(state[:2]))
        else:
            state = extended(jnp.concatenate([u, t, v]), 1, HALO)
            ux, tx, vx = (tiled(state[:2]), tiled(state[2:4]), tiled(state[4:]))
        for r in range(ROUNDS):
            first, last = (sweep == 0 and r == 0, sweep == SWEEPS - 1 and r == ROUNDS - 1)
            if not first:
                part = lax.all_to_all(part, axes, 0, 0)
            ux, vx, part = run_round(first, last, entries, devices, pull, part, ux, vx, tx, w)
        u = untiled(ux)[:, HALO:HALO + rows]
        v = untiled(vx)[:, HALO:HALO + rows]
    return (u[:, None], v[:, None])


def solution(mesh):
    return jax.shard_map(
        on_device,
        mesh=mesh,
        in_specs=(
            P(None, "sec", "strip", None),
            P(None, "sec", "strip", None),
            P("sec", "strip", None),
            P("sec", "strip", None),
            P("sec", "strip", None),
        ),
        out_specs=(P(None, "sec", "strip", None), P(None, "sec", "strip", None)),
        check_vma=False,
    )
```

```python
import functools

import jax
import jax.numpy as jnp
from jax import lax
from jax.experimental import pallas as pl
from jax.experimental.pallas import tpu as pltpu
from jax.sharding import PartitionSpec as P

SWEEPS = 2
ROUNDS = 2
SUBSTEPS = 4

SPRING = 1.0
COUPLING = 0.5
STEP_SIZE = 0.4
DAMPING = 0.9
SPEED_CAP = 0.05
EPSILON = 1e-06

LANES = 128
SUBS = 8
TILE = (SUBS, LANES)
HALO = ROUNDS * SUBSTEPS
SPRING_WEIGHT = 0.5 * SPRING * STEP_SIZE * STEP_SIZE
PULL_WEIGHT = COUPLING * STEP_SIZE * STEP_SIZE
VMEM = pl.BlockSpec(memory_space=pltpu.VMEM)


def natural_index(tile, row, h, planes):
    return pl.ds(tile * (planes * SUBS * SUBS) + h * SUBS + row, SUBS, stride=planes * SUBS)


def flag(condition):
    return jnp.where(condition, 1.0, 0.0).astype(jnp.float32)


def section_flags():
    s, n = (lax.axis_index("sec"), lax.axis_size("sec"))
    odd = flag(lax.rem(s, 2) == 1)
    return flag(s > 0), flag(s < n - 1), odd, flag(jnp.logical_or(lax.rem(s, 4) == 1, lax.rem(s, 4) == 2))


def send_rows(tiles):
    half = (tiles - 2) // 2
    return ((0, 1, 0, 0), (1, 1 + half, 1, 0), (1 + half, tiles - 1, 2, 0), (tiles - 1, tiles, 0, SUBS))


def store_sends(sends, buffer, row, rows_before, even_value, odd_value, i, h):
    eb, ob, em, o1, o2 = sends
    if buffer == 0:
        eb[i, row, h] = even_value
        ob[i, row, h] = odd_value
    elif buffer == 1:
        em[i, row, h] = even_value
        o1[i, row, h] = odd_value
    else:
        em[i, rows_before + row, h] = even_value
        o2[i, row, h] = odd_value


def prepare_kernel(u_ref, f_ref, fixed_ref, across_ref, down_ref, uo_ref, w_ref, fo_ref, *sends):
    planes = uo_ref.shape[2]
    rows = fo_ref.shape[1]
    tiles = rows // SUBS
    _, _, odd, _ = section_flags()
    even_cut = jnp.full(TILE, odd, jnp.float32)
    odd_cut = jnp.full(TILE, 1.0 - odd, jnp.float32)
    last_strip = lax.axis_index("strip") == lax.axis_size("strip") - 1
    lane = lax.broadcasted_iota(jnp.int32, TILE, 1)
    sub = lax.broadcasted_iota(jnp.int32, TILE, 0)
    last_column = jnp.logical_and(lane == LANES - 1, sub == SUBS - 1)
    before = sends[3].shape[1]

    def tile_rows(tile, buffer, base):
        for r in range(SUBS):
            row = tile * SUBS + r
            for h in range(planes):
                at = natural_index(tile, r, h, planes)
                for i in range(2):
                    u, f = (u_ref[i, at, :], f_ref[i, at, :])
                    uo_ref[i, HALO + row, h] = u
                    fo_ref[i, row, h] = f
                    store_sends(sends, buffer, base + r, before, u - even_cut * f, u - odd_cut * f, i, h)
                across = across_ref[at, :].astype(jnp.float32) * SPRING_WEIGHT
                if h == planes - 1:
                    across = jnp.where(last_column, 0.0, across)
                down = down_ref[at, :].astype(jnp.float32) * SPRING_WEIGHT
                if isinstance(tile, int) and tile == tiles - 1 and r == SUBS - 1:
                    down = jnp.where(last_strip, 0.0, down)
                w_ref[0, HALO + row, h] = across
                w_ref[1, HALO + row, h] = down
                w_ref[2, HALO + row, h] = 1.0 - fixed_ref[at, :].astype(jnp.float32)

    for begin, end, buffer, base in send_rows(tiles):
        if end - begin == 1:
            tile_rows(begin, buffer, base)
        else:
            def body(tile, carry, begin=begin, buffer=buffer):
                tile_rows(tile, buffer, (tile - begin) * SUBS)
                return carry
            lax.fori_loop(begin, end, body, 0)


def edge_kernel(first, even_ref, odd_ref, f_ref, u_ref, x_ref, top_ref, bottom_ref):
    planes = u_ref.shape[2]
    rows = f_ref.shape[1]
    has_below, _, _, _ = section_flags()
    fields = 3 if first else 2
    for out, base, at in ((top_ref, 0, 0), (bottom_ref, SUBS, rows - SUBS)):
        for r in range(SUBS):
            for h in range(planes):
                for i in range(2):
                    out[i, r, h] = u_ref[i, HALO + at + r, h]
                    t = even_ref[i, base + r, h] + odd_ref[i, base + r, h] + has_below * f_ref[i, at + r, h]
                    out[2 + i, r, h] = PULL_WEIGHT * t
                for i in range(fields):
                    out[4 + i, r, h] = x_ref[i, HALO + at + r, h]


def make_row(u_ref, w_ref, t_ref, pull):
    planes = u_ref.shape[2]
    lane = lax.broadcasted_iota(jnp.int32, TILE, 1)
    lane_first, lane_last = (lane == 0, lane == LANES - 1)
    hs = range(planes)

    def from_right(x):
        rolled = [pltpu.roll(x[h], LANES - 1, 1) for h in hs]
        following = rolled[1:] + [pltpu.roll(rolled[0], SUBS - 1, 0)]
        return [jnp.where(lane_last, following[h], rolled[h]) for h in hs]

    def from_left(x):
        rolled = [pltpu.roll(x[h], 1, 1) for h in hs]
        preceding = [pltpu.roll(rolled[-1], 1, 0)] + rolled[:-1]
        return [jnp.where(lane_first, preceding[h], rolled[h]) for h in hs]

    def load(r):
        return [[u_ref[i, r, h] for h in hs] for i in range(2)]

    def down_force(r, u, below):
        out = [[], []]
        for h in hs:
            dx = below[0][h] - u[0][h]
            dy = below[1][h] - u[1][h]
            ey = dy + 1.0
            q = (dx * dx + ey * ey - 1.0) * w_ref[1, r, h]
            out[0].append(q * dx)
            out[1].append(q * ey)
        return out

    def row(r, carry, speed, damp):
        u, g_above = carry
        below = load(r + 1)
        g = down_force(r, u, below)
        right = [from_right(u[i]) for i in range(2)]
        f = [[], []]
        for h in hs:
            ax = right[0][h] - u[0][h]
            ay = right[1][h] - u[1][h]
            ex = ax + 1.0
            t = (ex * ex + ay * ay - 1.0) * w_ref[0, r, h]
            f[0].append(t * ex)
            f[1].append(t * ay)
        left = [from_left(f[i]) for i in range(2)]
        new_u, new_v = ([[], []], [[], []])
        for i in range(2):
            for h in hs:
                a = (f[i][h] - left[i][h]) + (g[i][h] - g_above[i][h]) + (t_ref[i, r, h] - pull * u[i][h])
                if speed is not None:
                    a = a + damp * speed(i, r, h)
                v = w_ref[2, r, h] * a
                new_v[i].append(v)
                new_u[i].append(u[i][h] + v)
        return (below, g), new_u, new_v

    def start(r):
        u = load(r)
        return u, down_force(r - 1, load(r - 1), u)

    return row, start


def run_substep(k, u_src, u_ref, v_ref, w_ref, t_ref, pull, speed, damp, own, carry_more):
    rows_all, planes = (u_ref.shape[1], u_ref.shape[2])
    tiles = (rows_all - 2 * HALO) // SUBS
    row, start = make_row(u_src, w_ref, t_ref, pull)

    def put(r, new_u, new_v):
        for i in range(2):
            for h in range(planes):
                u_ref[i, r, h] = new_u[i][h]
                v_ref[i, r, h] = new_v[i][h]

    def flat(carry):
        return tuple(x for part in carry for field in part for x in field)

    def unflat(values):
        it = iter(values)
        return tuple([[next(it) for _ in range(planes)] for _ in range(2)] for _ in range(2))

    carry = start(k)
    for r in range(k, HALO):
        carry, new_u, new_v = row(r, carry, speed, damp)
        put(r, new_u, new_v)

    def body(place, tile, state):
        carry, more = (unflat(state[0]), state[1])
        for r in range(SUBS):
            at = HALO + tile * SUBS + r
            carry, new_u, new_v = row(at, carry, speed, damp)
            if own is None:
                put(at, new_u, new_v)
            else:
                more = own(place, tile, r, at, new_u, new_v, more, put)
        return flat(carry), more

    state = (flat(carry), carry_more)
    if own is not None and getattr(own, "segments", None):
        for begin, end, buffer, base in own.segments:
            segment = functools.partial(body, (begin, buffer, base))
            if end - begin == 1:
                state = segment(begin, state)
            else:
                state = lax.fori_loop(begin, end, segment, state)
    else:
        state = lax.fori_loop(0, tiles, functools.partial(body, None), state)
    carry = unflat(state[0])
    for r in range(rows_all - HALO, rows_all - k):
        carry, new_u, new_v = row(r, carry, speed, damp)
        put(r, new_u, new_v)
    return state[1]


def energy_own(place, tile, r, at, new_u, new_v, more, put):
    put(at, new_u, new_v)
    for h in range(len(new_v[0])):
        more = more + (new_v[0][h] * new_v[0][h] + new_v[1][h] * new_v[1][h])
    return more


def store_part(part_ref, acc):
    part_ref[...] = jnp.broadcast_to(jnp.sum(acc, 0, keepdims=True)[None], part_ref.shape)


def limited(part_ref, entries):
    power = jnp.sum(part_ref[...]) / (STEP_SIZE * STEP_SIZE)
    spread = jnp.sqrt(jnp.full(TILE, power / entries + EPSILON, jnp.float32))
    return DAMPING * jnp.minimum(1.0, SPEED_CAP / spread)


def pull_of():
    has_below, has_above, _, _ = section_flags()
    return jnp.full(TILE, PULL_WEIGHT * (has_below + has_above), jnp.float32)


def start_kernel(first, entries, *refs):
    if first:
        (u_in, w_in, f_ref, top, bottom, above, beneath, even, odd1, odd2, relay,
         u_ref, w_ref, t_ref, v_ref, part_out) = refs
        part_ref, v_in = (None, None)
    else:
        (u_in, v_in, w_ref, f_ref, top, bottom, above, beneath, even, odd1, odd2, relay, part_ref,
         u_ref, v_ref, t_ref, part_out) = refs
    rows_all, planes = (u_ref.shape[1], u_ref.shape[2])
    rows = rows_all - 2 * HALO
    tiles = rows // SUBS
    has_below, _, _, direct = section_flags()
    own_flow = jnp.full(TILE, has_below, jnp.float32)
    direct = jnp.full(TILE, direct, jnp.float32)
    for halo, at in ((above, 0), (beneath, rows_all - HALO)):
        for r in range(HALO):
            for h in range(planes):
                for i in range(2):
                    u_ref[i, at + r, h] = halo[i, r, h]
                    t_ref[i, at + r, h] = halo[2 + i, r, h]
                if first:
                    for i in range(3):
                        w_ref[i, at + r, h] = halo[4 + i, r, h]
    for edge, at in ((top, HALO), (bottom, rows_all - HALO - SUBS)):
        for r in range(SUBS):
            for h in range(planes):
                for i in range(2):
                    t_ref[i, at + r, h] = edge[2 + i, r, h]
    half = odd1.shape[1]

    def copy(tile, carry):
        for r in range(SUBS):
            at = HALO + tile * SUBS + r
            for h in range(planes):
                for i in range(2):
                    u_ref[i, at, h] = u_in[i, at, h]
                if first:
                    for i in range(3):
                        w_ref[i, at, h] = w_in[i, at, h]
        return carry

    lax.fori_loop(0, tiles, copy, 0)

    def targets(second):
        def body(tile, carry):
            for r in range(SUBS):
                at = tile * SUBS + r
                for h in range(planes):
                    for i in range(2):
                        if second:
                            t = odd2[i, at, h] * direct + relay[i, at, h]
                        else:
                            t = odd1[i, at, h]
                        main = at + (half if second else 0)
                        t = t + even[i, main, h] + own_flow * f_ref[i, SUBS + main, h]
                        t_ref[i, HALO + SUBS + main, h] = PULL_WEIGHT * t
            return carry
        return body

    lax.fori_loop(0, half // SUBS, targets(False), 0)
    lax.fori_loop(0, odd2.shape[1] // SUBS, targets(True), 0)
    pull = pull_of()
    damp0 = None if first else limited(part_ref, entries)
    speed = lambda i, r, h: v_ref[i, r, h]

    def speed_in(i, r, h):
        if isinstance(r, int) and r < HALO:
            return above[4 + i, r, h]
        if isinstance(r, int) and r >= rows_all - HALO:
            return beneath[4 + i, r - (rows_all - HALO), h]
        return v_in[i, r, h]

    for step in range(SUBSTEPS):
        final = step == SUBSTEPS - 1
        acc = run_substep(
            1 + step, u_ref, u_ref, v_ref, w_ref, t_ref, pull,
            None if first and step == 0 else speed_in if step == 0 else speed, damp0 if step == 0 else DAMPING,
            energy_own if final else None, jnp.zeros(TILE, jnp.float32) if final else 0,
        )
    store_part(part_out, acc)


class SendOwn:
    def __init__(self, segments, sends, f_ref, cuts):
        self.segments, self.sends, self.f_ref, self.cuts = (segments, sends, f_ref, cuts)

    def __call__(self, place, tile, r, at, new_u, new_v, more, put):
        begin, buffer, base = place
        more = energy_own(place, tile, r, at, new_u, new_v, more, put)
        row = base + r if buffer == 0 else (tile - begin) * SUBS + r
        for i in range(2):
            for h in range(len(new_u[0])):
                f = self.f_ref[i, tile * SUBS + r, h]
                u = new_u[i][h]
                store_sends(self.sends, buffer, row, self.sends[3].shape[1], u - self.cuts[0] * f, u - self.cuts[1] * f, i, h)
        return more


class LastOwn:
    def __init__(self, u_out, v_out):
        self.u_out, self.v_out = (u_out, v_out)

    def __call__(self, place, tile, r, at, new_u, new_v, more, put):
        planes = len(new_u[0])
        for i in range(2):
            for h in range(planes):
                where = natural_index(tile, r, h, planes)
                self.u_out[i, where, :] = new_u[i][h]
                self.v_out[i, where, :] = new_v[i][h] * (1.0 / STEP_SIZE)
        return more


def finish_kernel(last, entries, *refs):
    if last:
        u_in, v_in, t_ref, w_ref, part_ref, u_out, v_out, u_ref, v_ref = refs
    else:
        u_in, v_in, t_ref, w_ref, part_ref, f_ref, u_ref, v_ref, part_out, *sends = refs
    tiles = (u_ref.shape[1] - 2 * HALO) // SUBS
    pull = pull_of()
    damp0 = limited(part_ref, entries)
    if last:
        own = LastOwn(u_out, v_out)
    else:
        _, _, odd, _ = section_flags()
        cuts = (jnp.full(TILE, odd, jnp.float32), jnp.full(TILE, 1.0 - odd, jnp.float32))
        own = SendOwn(send_rows(tiles), sends, f_ref, cuts)
    speed_in = lambda i, r, h: v_in[i, r, h]
    speed = lambda i, r, h: v_ref[i, r, h]
    more = 0
    for step in range(SUBSTEPS):
        final = step == SUBSTEPS - 1
        more = run_substep(
            1 + SUBSTEPS + step, u_in if step == 0 else u_ref, u_ref, v_ref, w_ref, t_ref, pull, speed_in if step == 0 else speed,
            damp0 if step == 0 else DAMPING, own if final else None,
            jnp.zeros(TILE, jnp.float32) if final else 0,
        )
    if not last:
        store_part(part_out, more)


def call(kernel, outs, operands, cost=0):
    return pl.pallas_call(
        kernel,
        out_shape=tuple(jax.ShapeDtypeStruct(o, jnp.float32) for o in outs),
        in_specs=[VMEM] * len(operands),
        out_specs=tuple(VMEM for _ in outs),
        cost_estimate=pl.CostEstimate(flops=cost, bytes_accessed=cost, transcendentals=0),
        compiler_params=pltpu.CompilerParams(vmem_limit_bytes=8 << 20),
    )(*operands)


def pairs(ones):
    return [p for a, b in ones for p in ((a, b), (b, a))]


def exchange(sends):
    n = lax.axis_size("sec")
    eb, ob, em, o1, o2 = sends
    even = pairs([(i, i + 1) for i in range(0, n - 1, 2)])
    odd = [(i, i + 1) for i in range(1, n - 1, 2)]
    far = [(i, j) for i, j in odd if i % 4 == 3]
    near = pairs([p for p in odd if p not in far])
    out = [(i, i + 4) for i, j in far] + [(j, j - 4) for i, j in far]
    back = [(i + 4, j) for i, j in far] + [(j - 4, i) for i, j in far]
    rob = lax.ppermute(ob, "sec", pairs(odd))
    reb = lax.ppermute(eb, "sec", even)
    ro2 = lax.ppermute(o2, "sec", near + out)
    ro1 = lax.ppermute(o1, "sec", pairs(odd))
    rem = lax.ppermute(em, "sec", even)
    relay = lax.ppermute(ro2, "sec", back)
    return reb, rob, rem, ro1, ro2, relay


def viewed(x, planes):
    fields, rows, columns = x.shape
    x = x.reshape(fields, rows // SUBS, SUBS, columns // LANES, LANES).transpose(0, 1, 3, 2, 4)
    return x.reshape(fields, rows * columns // LANES, LANES)


def unviewed(x, rows, columns):
    x = x.reshape(x.shape[0], rows // SUBS, columns // LANES, SUBS, LANES).transpose(0, 1, 3, 2, 4)
    return x.reshape(x.shape[0], rows, columns)


def on_device(start_offsets, section_flow, fixed_nodes, links_across, links_down):
    axes = ("sec", "strip")
    sections, strips = (lax.axis_size("sec"), lax.axis_size("strip"))
    devices = sections * strips
    _, rows, columns = fixed_nodes.shape
    entries = 2.0 * sections * strips * rows * columns
    planes = columns // (SUBS * LANES)
    tiles = rows // SUBS
    wide = lambda fields, count: (fields, count, planes) + TILE
    half = (tiles - 2) // 2 * SUBS
    main = rows - 2 * SUBS
    send_shapes = [wide(2, 2 * SUBS), wide(2, 2 * SUBS), wide(2, main), wide(2, half), wide(2, main - half)]
    rows_all = rows + 2 * HALO
    full, part_shape = (wide(2, rows_all), (devices, 1, LANES))
    up = [(i, i + 1) for i in range(strips - 1)]
    dn = [(j, i) for i, j in up]
    natural = rows * columns // LANES
    u, w, f, *sends = call(
        prepare_kernel, [full, wide(3, rows_all), wide(2, rows)] + send_shapes,
        [viewed(start_offsets[:, 0], planes), viewed(section_flow[:, 0], planes), viewed(fixed_nodes, planes)[0],
         viewed(links_across, planes)[0], viewed(links_down, planes)[0]], cost=4 << 20,
    )
    v, part = (None, None)
    for sweep in range(SWEEPS):
        first, last = (sweep == 0, sweep == SWEEPS - 1)
        if not first:
            part = lax.all_to_all(part, axes, 0, 0)
        reb, rob, rem, ro1, ro2, relay = exchange(sends)
        fields = 7 if first else 6
        top, bottom = call(
            functools.partial(edge_kernel, first), [wide(fields, SUBS)] * 2, [reb, rob, f, u, w if first else v], cost=1 << 18,
        )
        above = lax.ppermute(bottom, "strip", up)
        beneath = lax.ppermute(top, "strip", dn)
        received = [f, top, bottom, above, beneath, rem, ro1, ro2, relay]
        if first:
            u, w, t, v, part = call(
                functools.partial(start_kernel, True, entries), [full, wide(3, rows_all), full, full, part_shape],
                [u, w] + received, cost=16 << 20,
            )
        else:
            u, v, t, part = call(
                functools.partial(start_kernel, False, entries), [full, full, full, part_shape],
                [u, v, w] + received + [part], cost=16 << 20,
            )
        part = lax.all_to_all(part, axes, 0, 0)
        if last:
            u, v, *_ = call(
                functools.partial(finish_kernel, True, entries), [(2, natural, LANES), (2, natural, LANES), full, full],
                [u, v, t, w, part], cost=16 << 20,
            )
        else:
            u, v, part, *sends = call(
                functools.partial(finish_kernel, False, entries), [full, full, part_shape] + send_shapes,
                [u, v, t, w, part, f], cost=16 << 20,
            )
    return (unviewed(u, rows, columns)[:, None], unviewed(v, rows, columns)[:, None])


def solution(mesh):
    return jax.shard_map(
        on_device,
        mesh=mesh,
        in_specs=(
            P(None, "sec", "strip", None),
            P(None, "sec", "strip", None),
            P("sec", "strip", None),
            P("sec", "strip", None),
            P("sec", "strip", None),
        ),
        out_specs=(P(None, "sec", "strip", None), P(None, "sec", "strip", None)),
        check_vma=False,
    )
```

```python
import functools

import jax
import jax.numpy as jnp
from jax import lax
from jax.experimental import pallas as pl
from jax.experimental.pallas import tpu as pltpu
from jax.sharding import PartitionSpec as P

SWEEPS = 2
ROUNDS = 2
SUBSTEPS = 4

SPRING = 1.0
COUPLING = 0.5
STEP_SIZE = 0.4
DAMPING = 0.9
SPEED_CAP = 0.05
EPSILON = 1e-06

LANES = 128
SUBS = 8
TILE = (SUBS, LANES)
HALO = ROUNDS * SUBSTEPS
SPRING_WEIGHT = 0.5 * SPRING * STEP_SIZE * STEP_SIZE
PULL_WEIGHT = COUPLING * STEP_SIZE * STEP_SIZE
VMEM = pl.BlockSpec(memory_space=pltpu.VMEM)


def natural_index(tile, row, h, planes):
    return pl.ds(tile * (planes * SUBS * SUBS) + h * SUBS + row, SUBS, stride=planes * SUBS)


def flag(condition):
    return jnp.where(condition, 1.0, 0.0).astype(jnp.float32)


def section_flags():
    s, n = (lax.axis_index("sec"), lax.axis_size("sec"))
    odd = flag(lax.rem(s, 2) == 1)
    return flag(s > 0), flag(s < n - 1), odd, flag(jnp.logical_or(lax.rem(s, 4) == 1, lax.rem(s, 4) == 2))


def send_rows(tiles):
    half = (tiles - 2) // 2
    return ((0, 1, 0, 0), (1, 1 + half, 1, 0), (1 + half, tiles - 1, 2, 0), (tiles - 1, tiles, 0, SUBS))


def store_sends(sends, buffer, row, rows_before, even_value, odd_value, i, h):
    eb, ob, em, o1, o2 = sends
    if buffer == 0:
        eb[i, row, h] = even_value
        ob[i, row, h] = odd_value
    elif buffer == 1:
        em[i, row, h] = even_value
        o1[i, row, h] = odd_value
    else:
        em[i, rows_before + row, h] = even_value
        o2[i, row, h] = odd_value


def prepare_kernel(u_ref, f_ref, uo_ref, fo_ref, *sends):
    planes = uo_ref.shape[2]
    tiles = fo_ref.shape[1] // SUBS
    _, _, odd, _ = section_flags()
    even_cut = jnp.full(TILE, odd, jnp.float32)
    odd_cut = jnp.full(TILE, 1.0 - odd, jnp.float32)
    before = sends[3].shape[1]

    def tile_rows(tile, buffer, base):
        for r in range(SUBS):
            row = tile * SUBS + r
            for h in range(planes):
                at = natural_index(tile, r, h, planes)
                for i in range(2):
                    u, f = (u_ref[i, at, :], f_ref[i, at, :])
                    uo_ref[i, HALO + row, h] = u
                    fo_ref[i, row, h] = f
                    store_sends(sends, buffer, base + r, before, u - even_cut * f, u - odd_cut * f, i, h)

    for begin, end, buffer, base in send_rows(tiles):
        if end - begin == 1:
            tile_rows(begin, buffer, base)
        else:
            def body(tile, carry, begin=begin, buffer=buffer):
                tile_rows(tile, buffer, (tile - begin) * SUBS)
                return carry
            lax.fori_loop(begin, end, body, 0)


def weights_kernel(fixed_ref, across_ref, down_ref, w_ref):
    planes = w_ref.shape[2]
    tiles = (w_ref.shape[1] - 2 * HALO) // SUBS
    last_strip = lax.axis_index("strip") == lax.axis_size("strip") - 1
    lane = lax.broadcasted_iota(jnp.int32, TILE, 1)
    sub = lax.broadcasted_iota(jnp.int32, TILE, 0)
    last_column = jnp.logical_and(lane == LANES - 1, sub == SUBS - 1)

    def body(tile, carry):
        for r in range(SUBS):
            row = HALO + tile * SUBS + r
            for h in range(planes):
                at = natural_index(tile, r, h, planes)
                across = across_ref[at, :].astype(jnp.float32) * SPRING_WEIGHT
                if h == planes - 1:
                    across = jnp.where(last_column, 0.0, across)
                w_ref[0, row, h] = across
                w_ref[1, row, h] = down_ref[at, :].astype(jnp.float32) * SPRING_WEIGHT
                w_ref[2, row, h] = 1.0 - fixed_ref[at, :].astype(jnp.float32)
        return carry

    lax.fori_loop(0, tiles, body, 0)
    bottom = w_ref.shape[1] - HALO - 1
    for h in range(planes):
        w_ref[1, bottom, h] = jnp.where(last_strip, 0.0, w_ref[1, bottom, h])


def edge_kernel(first, even_ref, odd_ref, f_ref, u_ref, x_ref, top_ref, bottom_ref):
    planes = u_ref.shape[2]
    rows = f_ref.shape[1]
    has_below, _, _, _ = section_flags()
    fields = 3 if first else 2
    for out, base, at in ((top_ref, 0, 0), (bottom_ref, SUBS, rows - SUBS)):
        for r in range(SUBS):
            for h in range(planes):
                for i in range(2):
                    out[i, r, h] = u_ref[i, HALO + at + r, h]
                    t = even_ref[i, base + r, h] + odd_ref[i, base + r, h] + has_below * f_ref[i, at + r, h]
                    out[2 + i, r, h] = PULL_WEIGHT * t
                for i in range(fields):
                    out[4 + i, r, h] = x_ref[i, HALO + at + r, h]


class Stages:
    def __init__(self, u_ref, v_ref, w_ref, t_ref, keep_ref, pull, damp):
        self.u, self.v, self.w, self.t, self.keep = (u_ref, v_ref, w_ref, t_ref, keep_ref)
        self.pull, self.damp = (pull, damp)
        self.hs = range(u_ref.shape[2])
        lane = lax.broadcasted_iota(jnp.int32, TILE, 1)
        self.lane_first, self.lane_last = (lane == 0, lane == LANES - 1)

    def load(self, r):
        return [[self.u[i, r, h] for h in self.hs] for i in range(2)]

    def from_right(self, x):
        rolled = [pltpu.roll(x[h], LANES - 1, 1) for h in self.hs]
        following = rolled[1:] + [pltpu.roll(rolled[0], SUBS - 1, 0)]
        return [jnp.where(self.lane_last, following[h], rolled[h]) for h in self.hs]

    def from_left(self, x):
        rolled = [pltpu.roll(x[h], 1, 1) for h in self.hs]
        preceding = [pltpu.roll(rolled[-1], 1, 0)] + rolled[:-1]
        return [jnp.where(self.lane_first, preceding[h], rolled[h]) for h in self.hs]

    def down_force(self, r, u, below):
        out = [[], []]
        for h in self.hs:
            dx = below[0][h] - u[0][h]
            dy = below[1][h] - u[1][h]
            ey = dy + 1.0
            q = (dx * dx + ey * ey - 1.0) * self.w[1, r, h]
            out[0].append(q * dx)
            out[1].append(q * ey)
        return out

    def forces(self, at, count, g_above):
        u = self.load(at)
        for b in range(count):
            r = at + b
            right = [self.from_right(u[i]) for i in range(2)]
            below = self.load(r + 1)
            g = self.down_force(r, u, below)
            for h in self.hs:
                ax = right[0][h] - u[0][h]
                ay = right[1][h] - u[1][h]
                ex = ax + 1.0
                t = (ex * ex + ay * ay - 1.0) * self.w[0, r, h]
                f = (t * ex, t * ay)
                for i in range(2):
                    a = (g[i][h] - g_above[i][h]) + (self.t[i, r, h] - self.pull * u[i][h])
                    if self.damp is not None:
                        a = a + self.damp * self.v[i, r, h]
                    self.keep[i, r, h] = f[i]
                    self.keep[2 + i, r, h] = a + f[i]
            u, g_above = (below, g)
        return g_above

    def update(self, at, count, more, own):
        for b in range(count):
            r = at + b
            new_u, new_v = ([[], []], [[], []])
            for i in range(2):
                left = self.from_left([self.keep[i, r, h] for h in self.hs])
                for h in self.hs:
                    v = self.w[2, r, h] * (self.keep[2 + i, r, h] - left[h])
                    new_v[i].append(v)
                    new_u[i].append(self.u[i, r, h] + v)
            more = own(r, new_u, new_v, more)
        return more


def run_substep(k, stages, more, edge_own, segments):
    rows_all, planes = (stages.u.shape[1], stages.u.shape[2])
    tiles = (rows_all - 2 * HALO) // SUBS
    extra = HALO - k
    flat = lambda g: tuple(x for field in g for x in field)

    def body(own, tile, state):
        g = [state[0][i * planes:(i + 1) * planes] for i in range(2)]
        at = HALO + tile * SUBS
        g = stages.forces(at + SUBS, SUBS, g)
        return flat(g), stages.update(at, SUBS, state[1], own)

    g = stages.down_force(k - 1, stages.load(k - 1), stages.load(k))
    g = stages.forces(k, extra + SUBS, g)
    state = (flat(g), more)
    for begin, end, own in segments:
        step = functools.partial(body, own)
        end = min(end, tiles - 1)
        if end - begin == 1:
            state = step(begin, state)
        elif end > begin:
            state = lax.fori_loop(begin, end, step, state)
    g = [state[0][i * planes:(i + 1) * planes] for i in range(2)]
    stages.forces(rows_all - HALO, extra, g)
    more = stages.update(rows_all - HALO - SUBS, SUBS, state[1], segments[-1][2])
    stages.update(k, extra, 0, edge_own)
    stages.update(rows_all - HALO, extra, 0, edge_own)
    return more


def storer(u_ref, v_ref, energy):
    def own(r, new_u, new_v, more):
        for i in range(2):
            for h in range(len(new_u[i])):
                u_ref[i, r, h] = new_u[i][h]
                v_ref[i, r, h] = new_v[i][h]
        if energy:
            for h in range(len(new_v[0])):
                more = more + (new_v[0][h] * new_v[0][h] + new_v[1][h] * new_v[1][h])
        return more
    return own


def store_part(part_ref, acc):
    part_ref[...] = jnp.broadcast_to(jnp.sum(acc, 0, keepdims=True)[None], part_ref.shape)


def limited(part_ref, entries):
    power = jnp.sum(part_ref[...]) / (STEP_SIZE * STEP_SIZE)
    spread = jnp.sqrt(jnp.full(TILE, power / entries + EPSILON, jnp.float32))
    return DAMPING * jnp.minimum(1.0, SPEED_CAP / spread)


def pull_of():
    has_below, has_above, _, _ = section_flags()
    return jnp.full(TILE, PULL_WEIGHT * (has_below + has_above), jnp.float32)


def start_kernel(first, entries, *refs):
    if first:
        (u_in, w_in, f_ref, top, bottom, above, beneath, even, odd1, odd2, relay,
         u_ref, w_ref, t_ref, v_ref, part_out, keep_ref) = refs
        part_ref, x_ref = (None, w_ref)
    else:
        (u_in, v_in, w_ref, f_ref, top, bottom, above, beneath, even, odd1, odd2, relay, part_ref,
         u_ref, v_ref, t_ref, part_out, keep_ref) = refs
        x_ref = v_ref
    rows_all, planes = (u_ref.shape[1], u_ref.shape[2])
    rows = rows_all - 2 * HALO
    tiles = rows // SUBS
    fields = 3 if first else 2
    has_below, _, _, direct = section_flags()
    own_flow = jnp.full(TILE, has_below, jnp.float32)
    direct = jnp.full(TILE, direct, jnp.float32)
    for halo, at in ((above, 0), (beneath, rows_all - HALO)):
        for r in range(HALO):
            for h in range(planes):
                for i in range(2):
                    u_ref[i, at + r, h] = halo[i, r, h]
                    t_ref[i, at + r, h] = halo[2 + i, r, h]
                for i in range(fields):
                    x_ref[i, at + r, h] = halo[4 + i, r, h]
    for edge, at in ((top, HALO), (bottom, rows_all - HALO - SUBS)):
        for r in range(SUBS):
            for h in range(planes):
                for i in range(2):
                    t_ref[i, at + r, h] = edge[2 + i, r, h]
    half = odd1.shape[1]

    def copy(tile, carry):
        for r in range(SUBS):
            at = HALO + tile * SUBS + r
            for h in range(planes):
                for i in range(2):
                    u_ref[i, at, h] = u_in[i, at, h]
                    if not first:
                        v_ref[i, at, h] = v_in[i, at, h]
                if first:
                    for i in range(3):
                        w_ref[i, at, h] = w_in[i, at, h]
        return carry

    lax.fori_loop(0, tiles, copy, 0)

    def targets(second):
        def body(tile, carry):
            for r in range(SUBS):
                at = tile * SUBS + r
                for h in range(planes):
                    for i in range(2):
                        if second:
                            t = odd2[i, at, h] * direct + relay[i, at, h]
                        else:
                            t = odd1[i, at, h]
                        main = at + (half if second else 0)
                        t = t + even[i, main, h] + own_flow * f_ref[i, SUBS + main, h]
                        t_ref[i, HALO + SUBS + main, h] = PULL_WEIGHT * t
            return carry
        return body

    lax.fori_loop(0, half // SUBS, targets(False), 0)
    lax.fori_loop(0, odd2.shape[1] // SUBS, targets(True), 0)
    pull = pull_of()
    damp0 = None if first else limited(part_ref, entries)
    for step in range(SUBSTEPS):
        damp = None if first and step == 0 else damp0 if step == 0 else DAMPING
        stages = Stages(u_ref, v_ref, w_ref, t_ref, keep_ref, pull, damp)
        plain = storer(u_ref, v_ref, False)
        if step < SUBSTEPS - 1:
            run_substep(1 + step, stages, 0, plain, ((0, tiles, plain),))
        else:
            counted = storer(u_ref, v_ref, True)
            acc = run_substep(1 + step, stages, jnp.zeros(TILE, jnp.float32), plain, ((0, tiles, counted),))
    store_part(part_out, acc)


def sender(store, sends, f_ref, cuts, buffer, base, begin):
    def own(r, new_u, new_v, more):
        more = store(r, new_u, new_v, more)
        q = r - HALO
        row = base + q - begin * SUBS
        for i in range(2):
            for h in range(len(new_u[0])):
                f, u = (f_ref[i, q, h], new_u[i][h])
                store_sends(sends, buffer, row, sends[3].shape[1], u - cuts[0] * f, u - cuts[1] * f, i, h)
        return more
    return own


def finish_kernel(last, entries, *refs):
    if last:
        u_in, v_in, t_ref, w_ref, part_ref, u_out, v_out, keep_ref, u_ref, v_ref, u_flat, v_flat = refs
    else:
        u_in, v_in, t_ref, w_ref, part_ref, f_ref, u_ref, v_ref, part_out, *sends, keep_ref = refs
    rows_all, planes = (u_ref.shape[1], u_ref.shape[2])
    tiles = (rows_all - 2 * HALO) // SUBS
    pull = pull_of()
    damp0 = limited(part_ref, entries)
    for step in range(SUBSTEPS):
        k = 1 + SUBSTEPS + step
        source = (u_in, v_in) if step == 0 else (u_ref, v_ref)
        stages = Stages(*source, w_ref, t_ref, keep_ref, pull, damp0 if step == 0 else DAMPING)
        if step < SUBSTEPS - 1:
            plain = storer(u_ref, v_ref, False)
            run_substep(k, stages, 0, plain, ((0, tiles, plain),))
        elif last:
            def own(r, new_u, new_v, more):
                for i in range(2):
                    for h in range(planes):
                        at = pl.ds(pl.multiple_of(((r - HALO) * planes + h) * SUBS, SUBS), SUBS)
                        u_flat[i, at, :] = new_u[i][h]
                        v_flat[i, at, :] = new_v[i][h]
                return more

            run_substep(k, stages, 0, own, ((0, tiles, own),))
        else:
            _, _, odd, _ = section_flags()
            cuts = (jnp.full(TILE, odd, jnp.float32), jnp.full(TILE, 1.0 - odd, jnp.float32))
            store = storer(u_ref, v_ref, True)
            segments = [
                (begin, end, sender(store, sends, f_ref, cuts, buffer, base, begin))
                for begin, end, buffer, base in send_rows(tiles)
            ]
            more = run_substep(k, stages, jnp.zeros(TILE, jnp.float32), store, segments)
    if not last:
        store_part(part_out, more)
        return

    def natural(tile, carry):
        for p in range(SUBS):
            for h in range(planes):
                for i in range(2):
                    at = pl.ds(tile * (SUBS * planes * SUBS) + h * SUBS + p, SUBS, stride=planes * SUBS)
                    out = pl.ds(pl.multiple_of((tile * planes * SUBS + p * planes + h) * SUBS, SUBS), SUBS)
                    u_out[i, out, :] = u_flat[i, at, :]
                    v_out[i, out, :] = v_flat[i, at, :] * (1.0 / STEP_SIZE)
        return carry

    lax.fori_loop(0, tiles, natural, 0)


def call(kernel, outs, operands, cost=0, scratch=()):
    return pl.pallas_call(
        kernel,
        out_shape=tuple(jax.ShapeDtypeStruct(o, jnp.float32) for o in outs),
        in_specs=[VMEM] * len(operands),
        out_specs=tuple(VMEM for _ in outs),
        scratch_shapes=[pltpu.VMEM(shape, jnp.float32) for shape in scratch],
        cost_estimate=pl.CostEstimate(flops=cost, bytes_accessed=cost, transcendentals=0),
        compiler_params=pltpu.CompilerParams(vmem_limit_bytes=20 << 20),
    )(*operands)


def pairs(ones):
    return [p for a, b in ones for p in ((a, b), (b, a))]


def exchange(sends):
    n = lax.axis_size("sec")
    eb, ob, em, o1, o2 = sends
    even = pairs([(i, i + 1) for i in range(0, n - 1, 2)])
    odd = [(i, i + 1) for i in range(1, n - 1, 2)]
    far = [(i, j) for i, j in odd if i % 4 == 3]
    near = pairs([p for p in odd if p not in far])
    out = [(i, i + 4) for i, j in far] + [(j, j - 4) for i, j in far]
    back = [(i + 4, j) for i, j in far] + [(j - 4, i) for i, j in far]
    rob = lax.ppermute(ob, "sec", pairs(odd))
    reb = lax.ppermute(eb, "sec", even)
    ro2 = lax.ppermute(o2, "sec", near + out)
    ro1 = lax.ppermute(o1, "sec", pairs(odd))
    rem = lax.ppermute(em, "sec", even)
    relay = lax.ppermute(ro2, "sec", back)
    return reb, rob, rem, ro1, ro2, relay


def viewed(x, planes):
    fields, rows, columns = x.shape
    x = x.reshape(fields, rows // SUBS, SUBS, columns // LANES, LANES).transpose(0, 1, 3, 2, 4)
    return x.reshape(fields, rows * columns // LANES, LANES)


def unviewed(x, rows, columns):
    x = x.reshape(x.shape[0], rows // SUBS, columns // LANES, SUBS, LANES).transpose(0, 1, 3, 2, 4)
    return x.reshape(x.shape[0], rows, columns)


def on_device(start_offsets, section_flow, fixed_nodes, links_across, links_down):
    axes = ("sec", "strip")
    sections, strips = (lax.axis_size("sec"), lax.axis_size("strip"))
    devices = sections * strips
    _, rows, columns = fixed_nodes.shape
    entries = 2.0 * sections * strips * rows * columns
    planes = columns // (SUBS * LANES)
    tiles = rows // SUBS
    wide = lambda fields, count: (fields, count, planes) + TILE
    half = (tiles - 2) // 2 * SUBS
    main = rows - 2 * SUBS
    send_shapes = [wide(2, 2 * SUBS), wide(2, 2 * SUBS), wide(2, main), wide(2, half), wide(2, main - half)]
    rows_all = rows + 2 * HALO
    full, keep, part_shape = (wide(2, rows_all), wide(4, rows_all), (devices, 1, LANES))
    up = [(i, i + 1) for i in range(strips - 1)]
    dn = [(j, i) for i, j in up]
    natural = rows * columns // LANES
    u, f, *sends = call(
        prepare_kernel, [full, wide(2, rows)] + send_shapes,
        [viewed(start_offsets[:, 0], planes), viewed(section_flow[:, 0], planes)], cost=4 << 20,
    )
    (w,) = call(
        weights_kernel, [wide(3, rows_all)],
        [viewed(x, planes)[0] for x in (fixed_nodes, links_across, links_down)], cost=4 << 20,
    )
    v, part = (None, None)
    for sweep in range(SWEEPS):
        first, last = (sweep == 0, sweep == SWEEPS - 1)
        if not first:
            part = lax.all_to_all(part, axes, 0, 0)
        reb, rob, rem, ro1, ro2, relay = exchange(sends)
        fields = 7 if first else 6
        top, bottom = call(
            functools.partial(edge_kernel, first), [wide(fields, SUBS)] * 2, [reb, rob, f, u, w if first else v], cost=1 << 18,
        )
        above = lax.ppermute(bottom, "strip", up)
        beneath = lax.ppermute(top, "strip", dn)
        received = [f, top, bottom, above, beneath, rem, ro1, ro2, relay]
        if first:
            u, w, t, v, part = call(
                functools.partial(start_kernel, True, entries), [full, wide(3, rows_all), full, full, part_shape],
                [u, w] + received, cost=16 << 20, scratch=[keep],
            )
        else:
            u, v, t, part = call(
                functools.partial(start_kernel, False, entries), [full, full, full, part_shape],
                [u, v, w] + received + [part], cost=16 << 20, scratch=[keep],
            )
        part = lax.all_to_all(part, axes, 0, 0)
        if last:
            u, v = call(
                functools.partial(finish_kernel, True, entries), [(2, natural, LANES)] * 2,
                [u, v, t, w, part], cost=16 << 20, scratch=[keep, full, full, (2, natural, LANES), (2, natural, LANES)],
            )
        else:
            u, v, part, *sends = call(
                functools.partial(finish_kernel, False, entries), [full, full, part_shape] + send_shapes,
                [u, v, t, w, part, f], cost=16 << 20, scratch=[keep],
            )
    return (unviewed(u, rows, columns)[:, None], unviewed(v, rows, columns)[:, None])


def solution(mesh):
    return jax.shard_map(
        on_device,
        mesh=mesh,
        in_specs=(
            P(None, "sec", "strip", None),
            P(None, "sec", "strip", None),
            P("sec", "strip", None),
            P("sec", "strip", None),
            P("sec", "strip", None),
        ),
        out_specs=(P(None, "sec", "strip", None), P(None, "sec", "strip", None)),
        check_vma=False,
    )
```

```python
import functools

import jax
import jax.numpy as jnp
from jax import lax
from jax.experimental import pallas as pl
from jax.experimental.pallas import tpu as pltpu
from jax.sharding import PartitionSpec as P

SWEEPS = 2
ROUNDS = 2
SUBSTEPS = 4

SPRING = 1.0
COUPLING = 0.5
STEP_SIZE = 0.4
DAMPING = 0.9
SPEED_CAP = 0.05
EPSILON = 1e-06

LANES = 128
SUBS = 8
TILE = (SUBS, LANES)
HALO = ROUNDS * SUBSTEPS
SPRING_WEIGHT = 0.5 * SPRING * STEP_SIZE * STEP_SIZE
PULL_WEIGHT = COUPLING * STEP_SIZE * STEP_SIZE
VMEM = pl.BlockSpec(memory_space=pltpu.VMEM)


def natural_index(tile, row, h, planes):
    return pl.ds(tile * (planes * SUBS * SUBS) + h * SUBS + row, SUBS, stride=planes * SUBS)


def flag(condition):
    return jnp.where(condition, 1.0, 0.0).astype(jnp.float32)


def section_flags():
    s, n = (lax.axis_index("sec"), lax.axis_size("sec"))
    odd = flag(lax.rem(s, 2) == 1)
    return flag(s > 0), flag(s < n - 1), odd, flag(jnp.logical_or(lax.rem(s, 4) == 1, lax.rem(s, 4) == 2))


def send_rows(tiles):
    half = (tiles - 2) // 2
    return ((0, 1, 0, 0), (1, 1 + half, 1, 0), (1 + half, tiles - 1, 2, 0), (tiles - 1, tiles, 0, SUBS))


def store_sends(sends, buffer, row, rows_before, even_value, odd_value, i, h):
    eb, ob, em, o1, o2 = sends
    if buffer == 0:
        eb[i, row, h] = even_value
        ob[i, row, h] = odd_value
    elif buffer == 1:
        em[i, row, h] = even_value
        o1[i, row, h] = odd_value
    else:
        em[i, rows_before + row, h] = even_value
        o2[i, row, h] = odd_value


def prepare_kernel(u_ref, f_ref, uo_ref, fo_ref, *sends):
    planes = uo_ref.shape[2]
    tiles = fo_ref.shape[1] // SUBS
    _, _, odd, _ = section_flags()
    even_cut = jnp.full(TILE, odd, jnp.float32)
    odd_cut = jnp.full(TILE, 1.0 - odd, jnp.float32)
    before = sends[3].shape[1]

    def tile_rows(tile, buffer, base):
        for r in range(SUBS):
            row = tile * SUBS + r
            for h in range(planes):
                at = natural_index(tile, r, h, planes)
                for i in range(2):
                    u, f = (u_ref[i, at, :], f_ref[i, at, :])
                    uo_ref[i, HALO + row, h] = u
                    fo_ref[i, row, h] = f
                    store_sends(sends, buffer, base + r, before, u - even_cut * f, u - odd_cut * f, i, h)

    for begin, end, buffer, base in send_rows(tiles):
        if end - begin == 1:
            tile_rows(begin, buffer, base)
        else:
            def body(tile, carry, begin=begin, buffer=buffer):
                tile_rows(tile, buffer, (tile - begin) * SUBS)
                return carry
            lax.fori_loop(begin, end, body, 0)


def weights_kernel(fixed_ref, across_ref, down_ref, w_ref):
    planes = w_ref.shape[2]
    tiles = (w_ref.shape[1] - 2 * HALO) // SUBS
    last_strip = lax.axis_index("strip") == lax.axis_size("strip") - 1
    lane = lax.broadcasted_iota(jnp.int32, TILE, 1)
    sub = lax.broadcasted_iota(jnp.int32, TILE, 0)
    last_column = jnp.logical_and(lane == LANES - 1, sub == SUBS - 1)

    def body(tile, carry):
        for r in range(SUBS):
            row = HALO + tile * SUBS + r
            for h in range(planes):
                at = natural_index(tile, r, h, planes)
                across = across_ref[at, :].astype(jnp.float32) * SPRING_WEIGHT
                if h == planes - 1:
                    across = jnp.where(last_column, 0.0, across)
                w_ref[0, row, h] = across
                w_ref[1, row, h] = down_ref[at, :].astype(jnp.float32) * SPRING_WEIGHT
                w_ref[2, row, h] = 1.0 - fixed_ref[at, :].astype(jnp.float32)
        return carry

    lax.fori_loop(0, tiles, body, 0)
    bottom = w_ref.shape[1] - HALO - 1
    for h in range(planes):
        w_ref[1, bottom, h] = jnp.where(last_strip, 0.0, w_ref[1, bottom, h])


def edge_kernel(first, even_ref, odd_ref, f_ref, u_ref, x_ref, *rest):
    top_ref, bottom_ref = rest[-2:]
    planes = u_ref.shape[2]
    rows = f_ref.shape[1]
    has_below, _, _, _ = section_flags()
    fields = 3 if first else 2
    for out, base, at in ((top_ref, 0, 0), (bottom_ref, SUBS, rows - SUBS)):
        for r in range(SUBS):
            for h in range(planes):
                for i in range(2):
                    out[i, r, h] = u_ref[i, HALO + at + r, h]
                    t = even_ref[i, base + r, h] + odd_ref[i, base + r, h] + has_below * f_ref[i, at + r, h]
                    out[2 + i, r, h] = PULL_WEIGHT * t
                for i in range(fields):
                    out[4 + i, r, h] = x_ref[i, HALO + at + r, h]


class Stages:
    def __init__(self, u_ref, v_ref, w_ref, t_ref, keep_ref, pull, damp):
        self.u, self.v, self.w, self.t, self.keep = (u_ref, v_ref, w_ref, t_ref, keep_ref)
        self.pull, self.damp = (pull, damp)
        self.hs = range(u_ref.shape[2])
        lane = lax.broadcasted_iota(jnp.int32, TILE, 1)
        self.lane_first, self.lane_last = (lane == 0, lane == LANES - 1)

    def load(self, r):
        return [[self.u[i, r, h] for h in self.hs] for i in range(2)]

    def from_right(self, x):
        rolled = [pltpu.roll(x[h], LANES - 1, 1) for h in self.hs]
        following = rolled[1:] + [pltpu.roll(rolled[0], SUBS - 1, 0)]
        return [jnp.where(self.lane_last, following[h], rolled[h]) for h in self.hs]

    def from_left(self, x):
        rolled = [pltpu.roll(x[h], 1, 1) for h in self.hs]
        preceding = [pltpu.roll(rolled[-1], 1, 0)] + rolled[:-1]
        return [jnp.where(self.lane_first, preceding[h], rolled[h]) for h in self.hs]

    def down_force(self, r, u, below):
        out = [[], []]
        for h in self.hs:
            dx = below[0][h] - u[0][h]
            dy = below[1][h] - u[1][h]
            ey = dy + 1.0
            q = (dx * dx + ey * ey - 1.0) * self.w[1, r, h]
            out[0].append(q * dx)
            out[1].append(q * ey)
        return out

    def forces(self, at, count, g_above):
        u = self.load(at)
        for b in range(count):
            r = at + b
            right = [self.from_right(u[i]) for i in range(2)]
            below = self.load(r + 1)
            g = self.down_force(r, u, below)
            for h in self.hs:
                ax = right[0][h] - u[0][h]
                ay = right[1][h] - u[1][h]
                ex = ax + 1.0
                t = (ex * ex + ay * ay - 1.0) * self.w[0, r, h]
                f = (t * ex, t * ay)
                for i in range(2):
                    a = (g[i][h] - g_above[i][h]) + (self.t[i, r, h] - self.pull * u[i][h])
                    if self.damp is not None:
                        a = a + self.damp * self.v[i, r, h]
                    self.keep[i, r, h] = f[i]
                    self.keep[2 + i, r, h] = a + f[i]
            u, g_above = (below, g)
        return g_above

    def update(self, at, count, more, own):
        for b in range(count):
            r = at + b
            new_u, new_v = ([[], []], [[], []])
            for i in range(2):
                left = self.from_left([self.keep[i, r, h] for h in self.hs])
                for h in self.hs:
                    v = self.w[2, r, h] * (self.keep[2 + i, r, h] - left[h])
                    new_v[i].append(v)
                    new_u[i].append(self.u[i, r, h] + v)
            more = own(r, new_u, new_v, more)
        return more


def run_substep(k, stages, more, edge_own, segments, after=None):
    rows_all, planes = (stages.u.shape[1], stages.u.shape[2])
    tiles = (rows_all - 2 * HALO) // SUBS
    extra = HALO - k
    flat = lambda g: tuple(x for field in g for x in field)

    def body(own, tile, state):
        g = [state[0][i * planes:(i + 1) * planes] for i in range(2)]
        at = HALO + tile * SUBS
        g = stages.forces(at + SUBS, SUBS, g)
        more = stages.update(at, SUBS, state[1], own)
        if after is not None:
            after(tile)
        return flat(g), more

    g = stages.down_force(k - 1, stages.load(k - 1), stages.load(k))
    g = stages.forces(k, extra + SUBS, g)
    state = (flat(g), more)
    for begin, end, own in segments:
        step = functools.partial(body, own)
        end = min(end, tiles - 1)
        if end - begin == 1:
            state = step(begin, state)
        elif end > begin:
            state = lax.fori_loop(begin, end, step, state)
    g = [state[0][i * planes:(i + 1) * planes] for i in range(2)]
    stages.forces(rows_all - HALO, extra, g)
    more = stages.update(rows_all - HALO - SUBS, SUBS, state[1], segments[-1][2])
    stages.update(k, extra, 0, edge_own)
    stages.update(rows_all - HALO, extra, 0, edge_own)
    return more


def storer(u_ref, v_ref, energy):
    def own(r, new_u, new_v, more):
        for i in range(2):
            for h in range(len(new_u[i])):
                u_ref[i, r, h] = new_u[i][h]
                v_ref[i, r, h] = new_v[i][h]
        if energy:
            for h in range(len(new_v[0])):
                more = more + (new_v[0][h] * new_v[0][h] + new_v[1][h] * new_v[1][h])
        return more
    return own


def store_part(part_ref, acc):
    part_ref[...] = jnp.broadcast_to(jnp.sum(acc, 0, keepdims=True)[None], part_ref.shape)


def limited(part_ref, entries):
    power = jnp.sum(part_ref[...]) / (STEP_SIZE * STEP_SIZE)
    spread = jnp.sqrt(jnp.full(TILE, power / entries + EPSILON, jnp.float32))
    return DAMPING * jnp.minimum(1.0, SPEED_CAP / spread)


def pull_of():
    has_below, has_above, _, _ = section_flags()
    return jnp.full(TILE, PULL_WEIGHT * (has_below + has_above), jnp.float32)


def start_kernel(first, entries, *refs):
    if first:
        (u_in, w_in, f_ref, top, bottom, above, beneath, even, odd1, odd2, relay,
         u_ref, w_ref, t_ref, v_ref, part_out, keep_ref) = refs
        part_ref, x_ref = (None, w_ref)
    else:
        (u_in, v_in, w_ref, f_ref, top, bottom, above, beneath, even, odd1, odd2, relay, part_ref,
         u_ref, v_ref, t_ref, part_out, keep_ref) = refs
        x_ref = v_ref
    rows_all, planes = (u_ref.shape[1], u_ref.shape[2])
    rows = rows_all - 2 * HALO
    tiles = rows // SUBS
    fields = 3 if first else 2
    has_below, _, _, direct = section_flags()
    own_flow = jnp.full(TILE, has_below, jnp.float32)
    direct = jnp.full(TILE, direct, jnp.float32)
    for halo, at in ((above, 0), (beneath, rows_all - HALO)):
        for r in range(HALO):
            for h in range(planes):
                for i in range(2):
                    u_ref[i, at + r, h] = halo[i, r, h]
                    t_ref[i, at + r, h] = halo[2 + i, r, h]
                for i in range(fields):
                    x_ref[i, at + r, h] = halo[4 + i, r, h]
    for edge, at in ((top, HALO), (bottom, rows_all - HALO - SUBS)):
        for r in range(SUBS):
            for h in range(planes):
                for i in range(2):
                    t_ref[i, at + r, h] = edge[2 + i, r, h]
    half = odd1.shape[1]

    def copy(tile, carry):
        for r in range(SUBS):
            at = HALO + tile * SUBS + r
            for h in range(planes):
                for i in range(2):
                    u_ref[i, at, h] = u_in[i, at, h]
                    if not first:
                        v_ref[i, at, h] = v_in[i, at, h]
                if first:
                    for i in range(3):
                        w_ref[i, at, h] = w_in[i, at, h]
        return carry

    lax.fori_loop(0, tiles, copy, 0)

    def targets(second):
        def body(tile, carry):
            for r in range(SUBS):
                at = tile * SUBS + r
                for h in range(planes):
                    for i in range(2):
                        if second:
                            t = odd2[i, at, h] * direct + relay[i, at, h]
                        else:
                            t = odd1[i, at, h]
                        main = at + (half if second else 0)
                        t = t + even[i, main, h] + own_flow * f_ref[i, SUBS + main, h]
                        t_ref[i, HALO + SUBS + main, h] = PULL_WEIGHT * t
            return carry
        return body

    lax.fori_loop(0, half // SUBS, targets(False), 0)
    lax.fori_loop(0, odd2.shape[1] // SUBS, targets(True), 0)
    pull = pull_of()
    damp0 = None if first else limited(part_ref, entries)
    for step in range(SUBSTEPS):
        damp = None if first and step == 0 else damp0 if step == 0 else DAMPING
        stages = Stages(u_ref, v_ref, w_ref, t_ref, keep_ref, pull, damp)
        plain = storer(u_ref, v_ref, False)
        if step < SUBSTEPS - 1:
            run_substep(1 + step, stages, 0, plain, ((0, tiles, plain),))
        else:
            counted = storer(u_ref, v_ref, True)
            acc = run_substep(1 + step, stages, jnp.zeros(TILE, jnp.float32), plain, ((0, tiles, counted),))
    store_part(part_out, acc)


def sender(store, sends, f_ref, cuts, buffer, base, begin):
    def own(r, new_u, new_v, more):
        more = store(r, new_u, new_v, more)
        q = r - HALO
        row = base + q - begin * SUBS
        for i in range(2):
            for h in range(len(new_u[0])):
                f, u = (f_ref[i, q, h], new_u[i][h])
                store_sends(sends, buffer, row, sends[3].shape[1], u - cuts[0] * f, u - cuts[1] * f, i, h)
        return more
    return own


def finish_kernel(last, entries, *refs):
    if last:
        u_in, v_in, t_ref, w_ref, part_ref, u_out, v_out, keep_ref, u_ref, v_ref, u_flat, v_flat, u_nat, v_nat, sems = refs
    else:
        u_in, v_in, t_ref, w_ref, part_ref, f_ref, u_ref, v_ref, part_out, *sends, keep_ref = refs
    rows_all, planes = (u_ref.shape[1], u_ref.shape[2])
    tiles = (rows_all - 2 * HALO) // SUBS
    pull = pull_of()
    damp0 = limited(part_ref, entries)
    lines = planes * SUBS * SUBS

    def turn(tile):
        for p in range(SUBS):
            for h in range(planes):
                for i in range(2):
                    at = pl.ds(tile * SUBS * SUBS + p, SUBS, stride=SUBS)
                    out = pl.ds(pl.multiple_of(tile * lines + (p * planes + h) * SUBS, SUBS), SUBS)
                    u_nat[i, out, :] = u_flat[i * planes + h, at, :]
                    v_nat[i, out, :] = v_flat[i * planes + h, at, :] * (1.0 / STEP_SIZE)

    def send(begin, count):
        at = pl.ds(pl.multiple_of(begin * lines, lines), count * lines)
        for i, (nat, out) in enumerate(((u_nat, u_out), (v_nat, v_out))):
            for field in range(2):
                pltpu.make_async_copy(nat.at[field, at, :], out.at[field, at, :], sems.at[i]).start()

    def turn_and_send(tile):
        turn(jnp.maximum(tile - 1, 0))

        @pl.when(tile >= 2)
        def _():
            send(tile - 2, 1)

    for step in range(SUBSTEPS):
        k = 1 + SUBSTEPS + step
        source = (u_in, v_in) if step == 0 else (u_ref, v_ref)
        stages = Stages(*source, w_ref, t_ref, keep_ref, pull, damp0 if step == 0 else DAMPING)
        if step < SUBSTEPS - 1:
            plain = storer(u_ref, v_ref, False)
            run_substep(k, stages, 0, plain, ((0, tiles, plain),))
        elif last:
            def own(r, new_u, new_v, more):
                for i in range(2):
                    for h in range(planes):
                        at = pl.ds(pl.multiple_of((r - HALO) * SUBS, SUBS), SUBS)
                        u_flat[i * planes + h, at, :] = new_u[i][h]
                        v_flat[i * planes + h, at, :] = new_v[i][h]
                return more

            run_substep(k, stages, 0, own, ((0, tiles, own),), turn_and_send)
        else:
            _, _, odd, _ = section_flags()
            cuts = (jnp.full(TILE, odd, jnp.float32), jnp.full(TILE, 1.0 - odd, jnp.float32))
            store = storer(u_ref, v_ref, True)
            segments = [
                (begin, end, sender(store, sends, f_ref, cuts, buffer, base, begin))
                for begin, end, buffer, base in send_rows(tiles)
            ]
            more = run_substep(k, stages, jnp.zeros(TILE, jnp.float32), store, segments)
    if not last:
        store_part(part_out, more)
        return

    for tile in range(tiles - 2, tiles):
        turn(tile)
    send(tiles - 3, 3)
    for i, (nat, out) in enumerate(((u_nat, u_out), (v_nat, v_out))):
        pltpu.make_async_copy(nat, out, sems.at[i]).wait()


def call(kernel, outs, operands, cost=0, scratch=(), copies=0):
    return pl.pallas_call(
        kernel,
        out_shape=tuple(jax.ShapeDtypeStruct(o, jnp.float32) for o in outs),
        in_specs=[VMEM] * len(operands),
        out_specs=tuple(pl.BlockSpec(memory_space=pl.ANY) if copies else VMEM for _ in outs),
        scratch_shapes=[pltpu.VMEM(shape, jnp.float32) for shape in scratch] + [pltpu.SemaphoreType.DMA((copies,))] * (copies > 0),
        cost_estimate=pl.CostEstimate(flops=cost, bytes_accessed=cost, transcendentals=0),
        compiler_params=pltpu.CompilerParams(vmem_limit_bytes=24 << 20),
    )(*operands)


def pairs(ones):
    return [p for a, b in ones for p in ((a, b), (b, a))]


def exchange(sends):
    n = lax.axis_size("sec")
    eb, ob, em, o1, o2 = sends
    even = pairs([(i, i + 1) for i in range(0, n - 1, 2)])
    odd = [(i, i + 1) for i in range(1, n - 1, 2)]
    far = [(i, j) for i, j in odd if i % 4 == 3]
    near = pairs([p for p in odd if p not in far])
    out = [(i, i + 4) for i, j in far] + [(j, j - 4) for i, j in far]
    back = [(i + 4, j) for i, j in far] + [(j - 4, i) for i, j in far]
    rob = lax.ppermute(ob, "sec", pairs(odd))
    reb = lax.ppermute(eb, "sec", even)
    ro2 = lax.ppermute(o2, "sec", near + out)
    ro1 = lax.ppermute(o1, "sec", pairs(odd))
    rem = lax.ppermute(em, "sec", even)
    relay = lax.ppermute(ro2, "sec", back)
    return reb, rob, rem, ro1, ro2, relay


def viewed(x, planes):
    fields, rows, columns = x.shape
    x = x.reshape(fields, rows // SUBS, SUBS, columns // LANES, LANES).transpose(0, 1, 3, 2, 4)
    return x.reshape(fields, rows * columns // LANES, LANES)


def unviewed(x, rows, columns):
    x = x.reshape(x.shape[0], rows // SUBS, columns // LANES, SUBS, LANES).transpose(0, 1, 3, 2, 4)
    return x.reshape(x.shape[0], rows, columns)


def on_device(start_offsets, section_flow, fixed_nodes, links_across, links_down):
    axes = ("sec", "strip")
    sections, strips = (lax.axis_size("sec"), lax.axis_size("strip"))
    devices = sections * strips
    _, rows, columns = fixed_nodes.shape
    entries = 2.0 * sections * strips * rows * columns
    planes = columns // (SUBS * LANES)
    tiles = rows // SUBS
    wide = lambda fields, count: (fields, count, planes) + TILE
    half = (tiles - 2) // 2 * SUBS
    main = rows - 2 * SUBS
    send_shapes = [wide(2, 2 * SUBS), wide(2, 2 * SUBS), wide(2, main), wide(2, half), wide(2, main - half)]
    rows_all = rows + 2 * HALO
    full, keep, part_shape = (wide(2, rows_all), wide(4, rows_all), (devices, 1, LANES))
    up = [(i, i + 1) for i in range(strips - 1)]
    dn = [(j, i) for i, j in up]
    natural = rows * columns // LANES
    u, f, *sends = call(
        prepare_kernel, [full, wide(2, rows)] + send_shapes,
        [viewed(start_offsets[:, 0], planes), viewed(section_flow[:, 0], planes)], cost=4 << 20,
    )
    (w,) = call(
        weights_kernel, [wide(3, rows_all)],
        [viewed(x, planes)[0] for x in (fixed_nodes, links_across, links_down)], cost=4 << 20,
    )
    v, part = (None, None)
    for sweep in range(SWEEPS):
        first, last = (sweep == 0, sweep == SWEEPS - 1)
        if not first:
            part = lax.all_to_all(part, axes, 0, 0)
        reb, rob, rem, ro1, ro2, relay = exchange(sends)
        fields = 7 if first else 6
        top, bottom = call(
            functools.partial(edge_kernel, first), [wide(fields, SUBS)] * 2, [reb, rob, f, u] + ([w] if first else [v, part]), cost=1 << 18,
        )
        above = lax.ppermute(bottom, "strip", up)
        beneath = lax.ppermute(top, "strip", dn)
        received = [f, top, bottom, above, beneath, rem, ro1, ro2, relay]
        if first:
            u, w, t, v, part = call(
                functools.partial(start_kernel, True, entries), [full, wide(3, rows_all), full, full, part_shape],
                [u, w] + received, cost=16 << 20, scratch=[keep],
            )
        else:
            u, v, t, part = call(
                functools.partial(start_kernel, False, entries), [full, full, full, part_shape],
                [u, v, w] + received + [part], cost=16 << 20, scratch=[keep],
            )
        part = lax.all_to_all(part, axes, 0, 0)
        if last:
            u, v = call(
                functools.partial(finish_kernel, True, entries), [(2, natural, LANES)] * 2,
                [u, v, t, w, part], cost=16 << 20, scratch=[keep, full, full] + [(2 * planes, rows * SUBS, LANES)] * 2 + [(2, natural, LANES)] * 2, copies=2,
            )
        else:
            u, v, part, *sends = call(
                functools.partial(finish_kernel, False, entries), [full, full, part_shape] + send_shapes,
                [u, v, t, w, part, f], cost=16 << 20, scratch=[keep],
            )
    return (unviewed(u, rows, columns)[:, None], unviewed(v, rows, columns)[:, None])


def solution(mesh):
    return jax.shard_map(
        on_device,
        mesh=mesh,
        in_specs=(
            P(None, "sec", "strip", None),
            P(None, "sec", "strip", None),
            P("sec", "strip", None),
            P("sec", "strip", None),
            P("sec", "strip", None),
        ),
        out_specs=(P(None, "sec", "strip", None), P(None, "sec", "strip", None)),
        check_vma=False,
    )
```

```python
import functools

import jax
import jax.numpy as jnp
from jax import lax
from jax.experimental import pallas as pl
from jax.experimental.pallas import tpu as pltpu
from jax.sharding import PartitionSpec as P


SWEEPS = 2
ROUNDS = 2
SUBSTEPS = 4

SPRING = 1.0
COUPLING = 0.5
STEP_SIZE = 0.4
DAMPING = 0.9
SPEED_CAP = 0.05
EPSILON = 1e-06


LANES = 128
SUBS = 8
TILE = (SUBS, LANES)
HALO = ROUNDS * SUBSTEPS
SPRING_WEIGHT = 0.5 * SPRING * STEP_SIZE * STEP_SIZE
PULL_WEIGHT = COUPLING * STEP_SIZE * STEP_SIZE
VMEM = pl.BlockSpec(memory_space=pltpu.VMEM)


def natural_index(tile, row, h, planes):
    return pl.ds(tile * (planes * SUBS * SUBS) + h * SUBS + row, SUBS, stride=planes * SUBS)


def flag(condition):
    return jnp.where(condition, 1.0, 0.0).astype(jnp.float32)


def section_flags():
    s, n = (lax.axis_index("sec"), lax.axis_size("sec"))
    odd = flag(lax.rem(s, 2) == 1)
    return flag(s > 0), flag(s < n - 1), odd


def send_rows(tiles):
    half = (tiles - 2) // 2
    return ((0, 1, 0, 0), (1, 1 + half, 1, 0), (1 + half, tiles - 1, 2, 0), (tiles - 1, tiles, 0, SUBS))


def store_sends(sends, buffer, row, rows_before, even_value, odd_value, i, h):
    eb, ob, em, o1, o2 = sends
    if buffer == 0:
        eb[i, row, h] = even_value
        ob[i, row, h] = odd_value
    elif buffer == 1:
        em[i, row, h] = even_value
        o1[i, row, h] = odd_value
    else:
        em[i, rows_before + row, h] = even_value
        o2[i, row, h] = odd_value


def prepare_kernel(u_ref, f_ref, uo_ref, fo_ref, *sends):
    planes = uo_ref.shape[2]
    tiles = fo_ref.shape[1] // SUBS
    _, _, odd = section_flags()
    even_cut = jnp.full(TILE, odd, jnp.float32)
    odd_cut = jnp.full(TILE, 1.0 - odd, jnp.float32)
    before = sends[3].shape[1]

    def tile_rows(tile, buffer, base):
        for r in range(SUBS):
            row = tile * SUBS + r
            for h in range(planes):
                at = natural_index(tile, r, h, planes)
                for i in range(2):
                    u, f = (u_ref[i, at, :], f_ref[i, at, :])
                    uo_ref[i, HALO + row, h] = u
                    fo_ref[i, row, h] = f
                    store_sends(sends, buffer, base + r, before, u - even_cut * f, u - odd_cut * f, i, h)

    for begin, end, buffer, base in send_rows(tiles):
        if end - begin == 1:
            tile_rows(begin, buffer, base)
        else:
            def body(tile, carry, begin=begin, buffer=buffer):
                tile_rows(tile, buffer, (tile - begin) * SUBS)
                return carry

            lax.fori_loop(begin, end, body, 0)


def weights_kernel(fixed_ref, across_ref, down_ref, w_ref):
    planes = w_ref.shape[2]
    tiles = (w_ref.shape[1] - 2 * HALO) // SUBS
    last_strip = lax.axis_index("strip") == lax.axis_size("strip") - 1
    lane = lax.broadcasted_iota(jnp.int32, TILE, 1)
    sub = lax.broadcasted_iota(jnp.int32, TILE, 0)
    last_column = jnp.logical_and(lane == LANES - 1, sub == SUBS - 1)

    def body(tile, carry):
        for r in range(SUBS):
            row = HALO + tile * SUBS + r
            for h in range(planes):
                at = natural_index(tile, r, h, planes)
                across = across_ref[at, :].astype(jnp.float32) * SPRING_WEIGHT
                if h == planes - 1:
                    across = jnp.where(last_column, 0.0, across)
                w_ref[0, row, h] = across
                w_ref[1, row, h] = down_ref[at, :].astype(jnp.float32) * SPRING_WEIGHT
                w_ref[2, row, h] = 1.0 - fixed_ref[at, :].astype(jnp.float32)
        return carry

    lax.fori_loop(0, tiles, body, 0)
    bottom = w_ref.shape[1] - HALO - 1
    for h in range(planes):
        w_ref[1, bottom, h] = jnp.where(last_strip, 0.0, w_ref[1, bottom, h])


def edge_kernel(first, even_ref, odd_ref, f_ref, u_ref, x_ref, *rest):
    top_ref, bottom_ref = rest[-2:]
    planes = u_ref.shape[2]
    rows = f_ref.shape[1]
    has_below, _, _ = section_flags()
    fields = 3 if first else 2
    for out, base, at in ((top_ref, 0, 0), (bottom_ref, SUBS, rows - SUBS)):
        for r in range(SUBS):
            for h in range(planes):
                for i in range(2):
                    out[i, r, h] = u_ref[i, HALO + at + r, h]
                    t = even_ref[i, base + r, h] + odd_ref[i, base + r, h] + has_below * f_ref[i, at + r, h]
                    out[2 + i, r, h] = PULL_WEIGHT * t
                for i in range(fields):
                    out[4 + i, r, h] = x_ref[i, HALO + at + r, h]


class Stages:
    def __init__(self, u_ref, v_ref, w_ref, t_ref, keep_ref, pull, damp):
        self.u, self.v, self.w, self.t, self.keep = (u_ref, v_ref, w_ref, t_ref, keep_ref)
        self.pull, self.damp = (pull, damp)
        self.hs = range(u_ref.shape[2])
        lane = lax.broadcasted_iota(jnp.int32, TILE, 1)
        self.lane_first, self.lane_last = (lane == 0, lane == LANES - 1)

    def load(self, r):
        return [[self.u[i, r, h] for h in self.hs] for i in range(2)]

    def from_right(self, x):
        rolled = [pltpu.roll(x[h], LANES - 1, 1) for h in self.hs]
        following = rolled[1:] + [pltpu.roll(rolled[0], SUBS - 1, 0)]
        return [jnp.where(self.lane_last, following[h], rolled[h]) for h in self.hs]

    def from_left(self, x):
        rolled = [pltpu.roll(x[h], 1, 1) for h in self.hs]
        preceding = [pltpu.roll(rolled[-1], 1, 0)] + rolled[:-1]
        return [jnp.where(self.lane_first, preceding[h], rolled[h]) for h in self.hs]

    def down_force(self, r, u, below):
        out = [[], []]
        for h in self.hs:
            dx = below[0][h] - u[0][h]
            dy = below[1][h] - u[1][h]
            ey = dy + 1.0
            q = (dx * dx + ey * ey - 1.0) * self.w[1, r, h]
            out[0].append(q * dx)
            out[1].append(q * ey)
        return out

    def forces(self, at, count, g_above):
        u = self.load(at)
        for b in range(count):
            r = at + b
            right = [self.from_right(u[i]) for i in range(2)]
            below = self.load(r + 1)
            g = self.down_force(r, u, below)
            for h in self.hs:
                ax = right[0][h] - u[0][h]
                ay = right[1][h] - u[1][h]
                ex = ax + 1.0
                t = (ex * ex + ay * ay - 1.0) * self.w[0, r, h]
                f = (t * ex, t * ay)
                for i in range(2):
                    a = (g[i][h] - g_above[i][h]) + (self.t[i, r, h] - self.pull * u[i][h])
                    if self.damp is not None:
                        a = a + self.damp * self.v[i, r, h]
                    self.keep[i, r, h] = f[i]
                    self.keep[2 + i, r, h] = a + f[i]
            u, g_above = (below, g)
        return g_above

    def update(self, at, count, more, own):
        for b in range(count):
            r = at + b
            new_u, new_v = ([[], []], [[], []])
            for i in range(2):
                left = self.from_left([self.keep[i, r, h] for h in self.hs])
                for h in self.hs:
                    v = self.w[2, r, h] * (self.keep[2 + i, r, h] - left[h])
                    new_v[i].append(v)
                    new_u[i].append(self.u[i, r, h] + v)
            more = own(r, new_u, new_v, more)
        return more


def run_substep(k, stages, more, edge_own, segments, after=None):
    rows_all, planes = (stages.u.shape[1], stages.u.shape[2])
    tiles = (rows_all - 2 * HALO) // SUBS
    extra = HALO - k
    flat = lambda g: tuple(x for field in g for x in field)

    def body(own, tile, state):
        g = [state[0][i * planes:(i + 1) * planes] for i in range(2)]
        at = HALO + tile * SUBS
        g = stages.forces(at + SUBS, SUBS, g)
        more = stages.update(at, SUBS, state[1], own)
        if after is not None:
            after(tile)
        return flat(g), more

    g = stages.down_force(k - 1, stages.load(k - 1), stages.load(k))
    g = stages.forces(k, extra + SUBS, g)
    state = (flat(g), more)
    for begin, end, own in segments:
        step = functools.partial(body, own)
        end = min(end, tiles - 1)
        if end - begin == 1:
            state = step(begin, state)
        elif end > begin:
            state = lax.fori_loop(begin, end, step, state)
    g = [state[0][i * planes:(i + 1) * planes] for i in range(2)]
    stages.forces(rows_all - HALO, extra, g)
    more = stages.update(rows_all - HALO - SUBS, SUBS, state[1], segments[-1][2])
    stages.update(k, extra, 0, edge_own)
    stages.update(rows_all - HALO, extra, 0, edge_own)
    return more


def storer(u_ref, v_ref, energy):
    def own(r, new_u, new_v, more):
        for i in range(2):
            for h in range(len(new_u[i])):
                u_ref[i, r, h] = new_u[i][h]
                v_ref[i, r, h] = new_v[i][h]
        if energy:
            for h in range(len(new_v[0])):
                more = more + (new_v[0][h] * new_v[0][h] + new_v[1][h] * new_v[1][h])
        return more

    return own


def store_part(part_ref, acc):
    part_ref[...] = jnp.broadcast_to(jnp.sum(acc, 0, keepdims=True)[None], part_ref.shape)


def limited(part_ref, entries):
    power = jnp.sum(part_ref[...]) / (STEP_SIZE * STEP_SIZE)
    spread = jnp.sqrt(jnp.full(TILE, power / entries + EPSILON, jnp.float32))
    return DAMPING * jnp.minimum(1.0, SPEED_CAP / spread)


def pull_of():
    has_below, has_above, _ = section_flags()
    return jnp.full(TILE, PULL_WEIGHT * (has_below + has_above), jnp.float32)


def start_kernel(first, entries, *refs):
    if first:
        (u_in, w_in, f_ref, top, bottom, above, beneath, even, odd1, odd2, relay,
         u_ref, w_ref, t_ref, v_ref, part_out, keep_ref) = refs
        part_ref, x_ref = (None, w_ref)
    else:
        (u_in, v_in, w_ref, f_ref, top, bottom, above, beneath, even, odd1, odd2, relay, part_ref,
         u_ref, v_ref, t_ref, part_out, keep_ref) = refs
        x_ref = v_ref
    rows_all, planes = (u_ref.shape[1], u_ref.shape[2])
    rows = rows_all - 2 * HALO
    tiles = rows // SUBS
    fields = 3 if first else 2
    has_below, _, _ = section_flags()
    own_flow = jnp.full(TILE, has_below, jnp.float32)
    for halo, at in ((above, 0), (beneath, rows_all - HALO)):
        for r in range(HALO):
            for h in range(planes):
                for i in range(2):
                    u_ref[i, at + r, h] = halo[i, r, h]
                    t_ref[i, at + r, h] = halo[2 + i, r, h]
                for i in range(fields):
                    x_ref[i, at + r, h] = halo[4 + i, r, h]
    for edge, at in ((top, HALO), (bottom, rows_all - HALO - SUBS)):
        for r in range(SUBS):
            for h in range(planes):
                for i in range(2):
                    t_ref[i, at + r, h] = edge[2 + i, r, h]
    half = odd1.shape[1]

    def copy(tile, carry):
        for r in range(SUBS):
            at = HALO + tile * SUBS + r
            for h in range(planes):
                for i in range(2):
                    u_ref[i, at, h] = u_in[i, at, h]
                    if not first:
                        v_ref[i, at, h] = v_in[i, at, h]
                if first:
                    for i in range(3):
                        w_ref[i, at, h] = w_in[i, at, h]
        return carry

    lax.fori_loop(0, tiles, copy, 0)

    def targets(second):
        def body(tile, carry):
            for r in range(SUBS):
                at = tile * SUBS + r
                for h in range(planes):
                    for i in range(2):
                        if second:
                            t = odd2[i, at, h] + relay[i, at, h]
                        else:
                            t = odd1[i, at, h]
                        main = at + (half if second else 0)
                        t = t + even[i, main, h] + own_flow * f_ref[i, SUBS + main, h]
                        t_ref[i, HALO + SUBS + main, h] = PULL_WEIGHT * t
            return carry

        return body

    lax.fori_loop(0, half // SUBS, targets(False), 0)
    lax.fori_loop(0, odd2.shape[1] // SUBS, targets(True), 0)
    pull = pull_of()
    damp0 = None if first else limited(part_ref, entries)
    for step in range(SUBSTEPS):
        damp = None if first and step == 0 else damp0 if step == 0 else DAMPING
        stages = Stages(u_ref, v_ref, w_ref, t_ref, keep_ref, pull, damp)
        plain = storer(u_ref, v_ref, False)
        if step < SUBSTEPS - 1:
            run_substep(1 + step, stages, 0, plain, ((0, tiles, plain),))
        else:
            counted = storer(u_ref, v_ref, True)
            acc = run_substep(1 + step, stages, jnp.zeros(TILE, jnp.float32), plain, ((0, tiles, counted),))
    store_part(part_out, acc)


def sender(store, sends, f_ref, cuts, buffer, base, begin):
    def own(r, new_u, new_v, more):
        more = store(r, new_u, new_v, more)
        q = r - HALO
        row = base + q - begin * SUBS
        for i in range(2):
            for h in range(len(new_u[0])):
                f, u = (f_ref[i, q, h], new_u[i][h])
                store_sends(sends, buffer, row, sends[3].shape[1], u - cuts[0] * f, u - cuts[1] * f, i, h)
        return more

    return own


def finish_kernel(last, entries, *refs):
    if last:
        u_in, v_in, t_ref, w_ref, part_ref, u_out, v_out, keep_ref, u_ref, v_ref, u_flat, v_flat, u_nat, v_nat, sems = refs
    else:
        u_in, v_in, t_ref, w_ref, part_ref, f_ref, u_ref, v_ref, part_out, *sends, keep_ref = refs
    rows_all, planes = (u_ref.shape[1], u_ref.shape[2])
    tiles = (rows_all - 2 * HALO) // SUBS
    pull = pull_of()
    damp0 = limited(part_ref, entries)
    lines = planes * SUBS * SUBS

    def turn(tile):
        for p in range(SUBS):
            for h in range(planes):
                for i in range(2):
                    at = pl.ds(tile * SUBS * SUBS + p, SUBS, stride=SUBS)
                    out = pl.ds(pl.multiple_of(tile * lines + (p * planes + h) * SUBS, SUBS), SUBS)
                    u_nat[i, out, :] = u_flat[i * planes + h, at, :]
                    v_nat[i, out, :] = v_flat[i * planes + h, at, :] * (1.0 / STEP_SIZE)

    def send(begin, count):
        at = pl.ds(pl.multiple_of(begin * lines, lines), count * lines)
        for i, (nat, out) in enumerate(((u_nat, u_out), (v_nat, v_out))):
            for field in range(2):
                pltpu.make_async_copy(nat.at[field, at, :], out.at[field, at, :], sems.at[i]).start()

    def turn_and_send(tile):
        turn(jnp.maximum(tile - 1, 0))

        @pl.when(tile >= 2)
        def _():
            send(tile - 2, 1)

    for step in range(SUBSTEPS):
        k = 1 + SUBSTEPS + step
        source = (u_in, v_in) if step == 0 else (u_ref, v_ref)
        stages = Stages(*source, w_ref, t_ref, keep_ref, pull, damp0 if step == 0 else DAMPING)
        if step < SUBSTEPS - 1:
            plain = storer(u_ref, v_ref, False)
            run_substep(k, stages, 0, plain, ((0, tiles, plain),))
        elif last:
            def own(r, new_u, new_v, more):
                for i in range(2):
                    for h in range(planes):
                        at = pl.ds(pl.multiple_of((r - HALO) * SUBS, SUBS), SUBS)
                        u_flat[i * planes + h, at, :] = new_u[i][h]
                        v_flat[i * planes + h, at, :] = new_v[i][h]
                return more

            run_substep(k, stages, 0, own, ((0, tiles, own),), turn_and_send)
        else:
            _, _, odd = section_flags()
            cuts = (jnp.full(TILE, odd, jnp.float32), jnp.full(TILE, 1.0 - odd, jnp.float32))
            store = storer(u_ref, v_ref, True)
            segments = [
                (begin, end, sender(store, sends, f_ref, cuts, buffer, base, begin))
                for begin, end, buffer, base in send_rows(tiles)
            ]
            more = run_substep(k, stages, jnp.zeros(TILE, jnp.float32), store, segments)
    if not last:
        store_part(part_out, more)
        return

    for tile in range(tiles - 2, tiles):
        turn(tile)
    send(tiles - 3, 3)
    for i, (nat, out) in enumerate(((u_nat, u_out), (v_nat, v_out))):
        pltpu.make_async_copy(nat, out, sems.at[i]).wait()


def call(kernel, outs, operands, cost=0, scratch=(), copies=0):
    return pl.pallas_call(
        kernel,
        out_shape=tuple(jax.ShapeDtypeStruct(o, jnp.float32) for o in outs),
        in_specs=[VMEM] * len(operands),
        out_specs=tuple(pl.BlockSpec(memory_space=pl.ANY) if copies else VMEM for _ in outs),
        scratch_shapes=[pltpu.VMEM(shape, jnp.float32) for shape in scratch] + [pltpu.SemaphoreType.DMA((copies,))] * (copies > 0),
        cost_estimate=pl.CostEstimate(flops=cost, bytes_accessed=cost, transcendentals=0),
        compiler_params=pltpu.CompilerParams(vmem_limit_bytes=24 << 20),
    )(*operands)


def pairs(ones):
    return [p for a, b in ones for p in ((a, b), (b, a))]


def exchange(sends):
    n = lax.axis_size("sec")
    eb, ob, em, o1, o2 = sends
    even = pairs([(i, i + 1) for i in range(0, n - 1, 2)])
    odd = [(i, i + 1) for i in range(1, n - 1, 2)]
    far = [(i, j) for i, j in odd if i % 4 == 3]
    near = pairs([p for p in odd if p not in far])
    out = [(i, i + 4) for i, j in far] + [(j, j - 4) for i, j in far]
    back = [(i + 4, j) for i, j in far] + [(j - 4, i) for i, j in far]

    rob = lax.ppermute(ob, "sec", pairs(odd))
    away = lax.ppermute(o2, "sec", out)
    ro1 = lax.ppermute(o1, "sec", pairs(odd))
    ro2 = lax.ppermute(o2, "sec", near)
    reb = lax.ppermute(eb, "sec", even)
    rem = lax.ppermute(em, "sec", even)
    relay = lax.ppermute(away, "sec", back)
    return reb, rob, rem, ro1, ro2, relay


def viewed(x):
    fields, rows, columns = x.shape
    x = x.reshape(fields, rows // SUBS, SUBS, columns // LANES, LANES).transpose(0, 1, 3, 2, 4)
    return x.reshape(fields, rows * columns // LANES, LANES)


def unviewed(x, rows, columns):
    x = x.reshape(x.shape[0], rows // SUBS, columns // LANES, SUBS, LANES).transpose(0, 1, 3, 2, 4)
    return x.reshape(x.shape[0], rows, columns)


def on_device(start_offsets, section_flow, fixed_nodes, links_across, links_down):
    axes = ("sec", "strip")
    sections, strips = (lax.axis_size("sec"), lax.axis_size("strip"))
    devices = sections * strips
    _, rows, columns = fixed_nodes.shape
    entries = 2.0 * sections * strips * rows * columns
    planes = columns // (SUBS * LANES)
    tiles = rows // SUBS
    wide = lambda fields, count: (fields, count, planes) + TILE
    half = (tiles - 2) // 2 * SUBS
    main = rows - 2 * SUBS
    send_shapes = [wide(2, 2 * SUBS), wide(2, 2 * SUBS), wide(2, main), wide(2, half), wide(2, main - half)]
    rows_all = rows + 2 * HALO
    full, keep, part_shape = (wide(2, rows_all), wide(4, rows_all), (devices, 1, LANES))
    up = [(i, i + 1) for i in range(strips - 1)]
    dn = [(j, i) for i, j in up]
    natural = rows * columns // LANES
    u, f, *sends = call(
        prepare_kernel, [full, wide(2, rows)] + send_shapes,
        [viewed(start_offsets[:, 0]), viewed(section_flow[:, 0])], cost=4 << 20,
    )
    (w,) = call(
        weights_kernel, [wide(3, rows_all)],
        [viewed(x)[0] for x in (fixed_nodes, links_across, links_down)], cost=4 << 20,
    )
    v, part = (None, None)
    for sweep in range(SWEEPS):
        first, last = (sweep == 0, sweep == SWEEPS - 1)
        if not first:
            part = lax.all_to_all(part, axes, 0, 0)
        reb, rob, rem, ro1, ro2, relay = exchange(sends)
        fields = 7 if first else 6
        top, bottom = call(
            functools.partial(edge_kernel, first), [wide(fields, SUBS)] * 2, [reb, rob, f, u, w if first else v], cost=1 << 18,
        )
        above = lax.ppermute(bottom, "strip", up)
        beneath = lax.ppermute(top, "strip", dn)
        received = [f, top, bottom, above, beneath, rem, ro1, ro2, relay]
        if first:
            u, w, t, v, part = call(
                functools.partial(start_kernel, True, entries), [full, wide(3, rows_all), full, full, part_shape],
                [u, w] + received, cost=16 << 20, scratch=[keep],
            )
        else:
            u, v, t, part = call(
                functools.partial(start_kernel, False, entries), [full, full, full, part_shape],
                [u, v, w] + received + [part], cost=16 << 20, scratch=[keep],
            )
        part = lax.all_to_all(part, axes, 0, 0)
        if last:
            u, v = call(
                functools.partial(finish_kernel, True, entries), [(2, natural, LANES)] * 2,
                [u, v, t, w, part], cost=16 << 20, scratch=[keep, full, full] + [(2 * planes, rows * SUBS, LANES)] * 2 + [(2, natural, LANES)] * 2, copies=2,
            )
        else:
            u, v, part, *sends = call(
                functools.partial(finish_kernel, False, entries), [full, full, part_shape] + send_shapes,
                [u, v, t, w, part, f], cost=16 << 20, scratch=[keep],
            )
    return (unviewed(u, rows, columns)[:, None], unviewed(v, rows, columns)[:, None])


def solution(mesh):
    return jax.shard_map(
        on_device,
        mesh=mesh,
        in_specs=(
            P(None, "sec", "strip", None),
            P(None, "sec", "strip", None),
            P("sec", "strip", None),
            P("sec", "strip", None),
            P("sec", "strip", None),
        ),
        out_specs=(P(None, "sec", "strip", None), P(None, "sec", "strip", None)),
        check_vma=False,
    )
```

```python
import functools

import jax
import jax.numpy as jnp
from jax import lax
from jax.experimental import pallas as pl
from jax.experimental.pallas import tpu as pltpu
from jax.sharding import PartitionSpec as P


SWEEPS = 2
ROUNDS = 2
SUBSTEPS = 4

SPRING = 1.0
COUPLING = 0.5
STEP_SIZE = 0.4
DAMPING = 0.9
SPEED_CAP = 0.05
EPSILON = 1e-06


LANES = 128
SUBS = 8
TILE = (SUBS, LANES)
HALO = ROUNDS * SUBSTEPS
SPRING_WEIGHT = 0.5 * SPRING * STEP_SIZE * STEP_SIZE
PULL_WEIGHT = COUPLING * STEP_SIZE * STEP_SIZE
VMEM = pl.BlockSpec(memory_space=pltpu.VMEM)


def natural_index(tile, row, h, planes):
    return pl.ds(tile * (planes * SUBS * SUBS) + h * SUBS + row, SUBS, stride=planes * SUBS)


def flag(condition):
    return jnp.where(condition, 1.0, 0.0).astype(jnp.float32)


def section_flags():
    s, n = (lax.axis_index("sec"), lax.axis_size("sec"))
    odd = flag(lax.rem(s, 2) == 1)
    return flag(s > 0), flag(s < n - 1), odd


def send_rows(tiles):
    half = (tiles - 2) // 2
    return ((0, 1, 0, 0), (1, 1 + half, 1, 0), (1 + half, tiles - 1, 2, 0), (tiles - 1, tiles, 0, SUBS))


def store_sends(sends, buffer, row, rows_before, even_value, odd_value, i, h):
    eb, ob, em, o1, o2 = sends
    if buffer == 0:
        eb[i, row, h] = even_value
        ob[i, row, h] = odd_value
    elif buffer == 1:
        em[i, row, h] = even_value
        o1[i, row, h] = odd_value
    else:
        em[i, rows_before + row, h] = even_value
        o2[i, row, h] = odd_value


def prepare_kernel(u_ref, f_ref, uo_ref, fo_ref, *sends):
    planes = uo_ref.shape[2]
    tiles = fo_ref.shape[1] // SUBS
    _, _, odd = section_flags()
    even_cut = jnp.full(TILE, odd, jnp.float32)
    odd_cut = jnp.full(TILE, 1.0 - odd, jnp.float32)
    before = sends[3].shape[1]

    def tile_rows(tile, buffer, base):
        for r in range(SUBS):
            row = tile * SUBS + r
            for h in range(planes):
                at = natural_index(tile, r, h, planes)
                for i in range(2):
                    u, f = (u_ref[i, at, :], f_ref[i, at, :])
                    uo_ref[i, HALO + row, h] = u
                    fo_ref[i, row, h] = f
                    store_sends(sends, buffer, base + r, before, u - even_cut * f, u - odd_cut * f, i, h)

    for begin, end, buffer, base in send_rows(tiles):
        if end - begin == 1:
            tile_rows(begin, buffer, base)
        else:
            def body(tile, carry, begin=begin, buffer=buffer):
                tile_rows(tile, buffer, (tile - begin) * SUBS)
                return carry

            lax.fori_loop(begin, end, body, 0)


def weights_kernel(fixed_ref, across_ref, down_ref, w_ref):
    planes = w_ref.shape[2]
    tiles = (w_ref.shape[1] - 2 * HALO) // SUBS
    last_strip = lax.axis_index("strip") == lax.axis_size("strip") - 1
    lane = lax.broadcasted_iota(jnp.int32, TILE, 1)
    sub = lax.broadcasted_iota(jnp.int32, TILE, 0)
    last_column = jnp.logical_and(lane == LANES - 1, sub == SUBS - 1)

    def body(tile, carry):
        for r in range(SUBS):
            row = HALO + tile * SUBS + r
            for h in range(planes):
                at = natural_index(tile, r, h, planes)
                across = across_ref[at, :].astype(jnp.float32) * SPRING_WEIGHT
                if h == planes - 1:
                    across = jnp.where(last_column, 0.0, across)
                w_ref[0, row, h] = across
                w_ref[1, row, h] = down_ref[at, :].astype(jnp.float32) * SPRING_WEIGHT
                w_ref[2, row, h] = 1.0 - fixed_ref[at, :].astype(jnp.float32)
        return carry

    lax.fori_loop(0, tiles, body, 0)
    bottom = w_ref.shape[1] - HALO - 1
    for h in range(planes):
        w_ref[1, bottom, h] = jnp.where(last_strip, 0.0, w_ref[1, bottom, h])


def edge_kernel(first, even_ref, odd_ref, f_ref, u_ref, x_ref, *rest):
    top_ref, bottom_ref = rest[-2:]
    planes = u_ref.shape[2]
    rows = f_ref.shape[1]
    has_below, _, _ = section_flags()
    fields = 3 if first else 2
    for out, base, at in ((top_ref, 0, 0), (bottom_ref, SUBS, rows - SUBS)):
        for r in range(SUBS):
            for h in range(planes):
                for i in range(2):
                    out[i, r, h] = u_ref[i, HALO + at + r, h]
                    t = even_ref[i, base + r, h] + odd_ref[i, base + r, h] + has_below * f_ref[i, at + r, h]
                    out[2 + i, r, h] = PULL_WEIGHT * t
                for i in range(fields):
                    out[4 + i, r, h] = x_ref[i, HALO + at + r, h]


class Stages:
    def __init__(self, u_ref, v_ref, w_ref, t_ref, keep_ref, pull, damp):
        self.u, self.v, self.w, self.t, self.keep = (u_ref, v_ref, w_ref, t_ref, keep_ref)
        self.pull, self.damp = (pull, damp)
        self.hs = range(u_ref.shape[2])
        lane = lax.broadcasted_iota(jnp.int32, TILE, 1)
        self.lane_first, self.lane_last = (lane == 0, lane == LANES - 1)

    def load(self, r):
        return [[self.u[i, r, h] for h in self.hs] for i in range(2)]

    def from_right(self, x):
        rolled = [pltpu.roll(x[h], LANES - 1, 1) for h in self.hs]
        following = rolled[1:] + [pltpu.roll(rolled[0], SUBS - 1, 0)]
        return [jnp.where(self.lane_last, following[h], rolled[h]) for h in self.hs]

    def from_left(self, x):
        rolled = [pltpu.roll(x[h], 1, 1) for h in self.hs]
        preceding = [pltpu.roll(rolled[-1], 1, 0)] + rolled[:-1]
        return [jnp.where(self.lane_first, preceding[h], rolled[h]) for h in self.hs]

    def down_force(self, r, u, below):
        out = [[], []]
        for h in self.hs:
            dx = below[0][h] - u[0][h]
            dy = below[1][h] - u[1][h]
            ey = dy + 1.0
            q = (dx * dx + ey * ey - 1.0) * self.w[1, r, h]
            out[0].append(q * dx)
            out[1].append(q * ey)
        return out

    def forces(self, at, count, g_above):
        u = self.load(at)
        for b in range(count):
            r = at + b
            right = [self.from_right(u[i]) for i in range(2)]
            below = self.load(r + 1)
            g = self.down_force(r, u, below)
            for h in self.hs:
                ax = right[0][h] - u[0][h]
                ay = right[1][h] - u[1][h]
                ex = ax + 1.0
                t = (ex * ex + ay * ay - 1.0) * self.w[0, r, h]
                f = (t * ex, t * ay)
                for i in range(2):
                    a = (g[i][h] - g_above[i][h]) + (self.t[i, r, h] - self.pull * u[i][h])
                    if self.damp is not None:
                        a = a + self.damp * self.v[i, r, h]
                    self.keep[i, r, h] = f[i]
                    self.keep[2 + i, r, h] = a + f[i]
            u, g_above = (below, g)
        return g_above

    def update(self, at, count, more, own):
        for b in range(count):
            r = at + b
            new_u, new_v = ([[], []], [[], []])
            for i in range(2):
                left = self.from_left([self.keep[i, r, h] for h in self.hs])
                for h in self.hs:
                    v = self.w[2, r, h] * (self.keep[2 + i, r, h] - left[h])
                    new_v[i].append(v)
                    new_u[i].append(self.u[i, r, h] + v)
            more = own(r, new_u, new_v, more)
        return more


def run_substep(k, stages, more, segments, head_own, tail_own, after=None, rows=None, g=None):
    rows_all, planes = (stages.u.shape[1], stages.u.shape[2])
    low, high = rows or (k, rows_all - k)
    first_row, last_row = (HALO + segments[0][0] * SUBS, HALO + segments[-1][1] * SUBS)
    head, tail = (first_row - low, high - last_row)
    flat = lambda g: tuple(x for field in g for x in field)
    unflat = lambda g: [g[i * planes:(i + 1) * planes] for i in range(2)]

    def body(own, tile, state):
        at = HALO + tile * SUBS
        g = stages.forces(at + SUBS, SUBS, unflat(state[0]))
        more = stages.update(at, SUBS, state[1], own)
        if after is not None:
            after(tile)
        return flat(g), more

    if g is None:
        g = stages.down_force(low - 1, stages.load(low - 1), stages.load(low))
    g = stages.forces(low, head + SUBS, g)
    state = (flat(g), more)
    for begin, end, own in segments:
        step = functools.partial(body, own)
        end = min(end, segments[-1][1] - 1)
        if end - begin == 1:
            state = step(begin, state)
        elif end > begin:
            state = lax.fori_loop(begin, end, step, state)
    g = stages.forces(last_row, tail, unflat(state[0]))
    more = stages.update(last_row - SUBS, SUBS, state[1], segments[-1][2])
    more = stages.update(low, head, more, head_own)
    more = stages.update(last_row, tail, more, tail_own)
    return more, g


def storer(u_ref, v_ref, energy):
    def own(r, new_u, new_v, more):
        for i in range(2):
            for h in range(len(new_u[i])):
                u_ref[i, r, h] = new_u[i][h]
                v_ref[i, r, h] = new_v[i][h]
        if energy:
            for h in range(len(new_v[0])):
                more = more + (new_v[0][h] * new_v[0][h] + new_v[1][h] * new_v[1][h])
        return more

    return own


def store_part(part_ref, acc):
    part_ref[...] = jnp.broadcast_to(jnp.sum(acc, 0, keepdims=True)[None], part_ref.shape)


def limited(part_ref, entries):
    power = jnp.sum(part_ref[...]) / (STEP_SIZE * STEP_SIZE)
    spread = jnp.sqrt(jnp.full(TILE, power / entries + EPSILON, jnp.float32))
    return DAMPING * jnp.minimum(1.0, SPEED_CAP / spread)


def pull_of():
    has_below, has_above, _ = section_flags()
    return jnp.full(TILE, PULL_WEIGHT * (has_below + has_above), jnp.float32)


def lay_halo(halo, at, refs):
    for field, ref, count in refs:
        for r in range(HALO):
            for h in range(ref.shape[2]):
                for i in range(count):
                    ref[i, at + r, h] = halo[field + i, r, h]


def lay_targets(t_ref, f_ref, even, odd, relay, begin):
    planes = t_ref.shape[2]
    has_below, _, _ = section_flags()
    own_flow = jnp.full(TILE, has_below, jnp.float32)

    def body(tile, carry):
        for r in range(SUBS):
            at = tile * SUBS + r
            main = at + begin
            for h in range(planes):
                for i in range(2):
                    t = odd[i, at, h]
                    if relay is not None:
                        t = t + relay[i, at, h]
                    t = t + even[i, main, h] + own_flow * f_ref[i, SUBS + main, h]
                    t_ref[i, HALO + SUBS + main, h] = PULL_WEIGHT * t
        return carry

    lax.fori_loop(0, odd.shape[1] // SUBS, body, 0)


def copy_rows(begin, end, pairs_of):
    def body(tile, carry):
        for source, target in pairs_of:
            for r in range(SUBS):
                for h in range(target.shape[2]):
                    for i in range(target.shape[0]):
                        target[i, tile * SUBS + r, h] = source[i, tile * SUBS + r, h]
        return carry

    lax.fori_loop(begin // SUBS, end // SUBS, body, 0)


def lay_edges(t_ref, top, bottom):
    rows_all = t_ref.shape[1]
    for edge, at in ((top, HALO), (bottom, rows_all - HALO - SUBS)):
        for r in range(SUBS):
            for h in range(t_ref.shape[2]):
                for i in range(2):
                    t_ref[i, at + r, h] = edge[2 + i, r, h]


def early_kernel(u_in, w_in, f_ref, top, bottom, above, beneath, even, odd1, u_ref, w_ref, t_ref, v_ref, g_ref, acc_ref, keep_ref):
    rows_all, planes = (u_ref.shape[1], u_ref.shape[2])
    for halo, at in ((above, 0), (beneath, rows_all - HALO)):
        lay_halo(halo, at, ((0, u_ref, 2), (2, t_ref, 2), (4, w_ref, 3)))
    lay_edges(t_ref, top, bottom)
    copy_rows(HALO, rows_all - HALO, ((u_in, u_ref), (w_in, w_ref)))
    lay_targets(t_ref, f_ref, even, odd1, None, 0)
    end = HALO + SUBS + odd1.shape[1]
    pull = pull_of()
    plain, counted = (storer(u_ref, v_ref, False), storer(u_ref, v_ref, True))
    for step in range(SUBSTEPS):
        k = 1 + step
        final = step == SUBSTEPS - 1
        stages = Stages(u_ref, v_ref, w_ref, t_ref, keep_ref, pull, DAMPING if step else None)
        own = counted if final else plain
        acc, g = run_substep(
            k, stages, jnp.zeros(TILE, jnp.float32) if final else 0, ((0, (end - k - HALO) // SUBS, own),),
            plain, own, rows=(k, end - k),
        )
        for i in range(2):
            for h in range(planes):
                g_ref[step, i, h] = g[i][h]
    acc_ref[...] = acc


def late_kernel(u_in, w_ref, t_in, v_in, g_ref, acc_ref, f_ref, even, odd2, relay, u_ref, t_ref, v_ref, part_out, keep_ref):
    rows_all, planes = (u_ref.shape[1], u_ref.shape[2])
    begin = rows_all - HALO - SUBS - odd2.shape[1]
    copy_rows(0, rows_all, ((u_in, u_ref),))
    copy_rows(0, begin, ((v_in, v_ref), (t_in, t_ref)))
    copy_rows(rows_all - HALO - SUBS, rows_all, ((t_in, t_ref),))
    lay_targets(t_ref, f_ref, even, odd2, relay, begin - HALO - SUBS)
    pull = pull_of()
    plain, counted = (storer(u_ref, v_ref, False), storer(u_ref, v_ref, True))
    tiles = (rows_all - 2 * HALO) // SUBS
    for step in range(SUBSTEPS):
        k = 1 + step
        final = step == SUBSTEPS - 1
        stages = Stages(u_ref, v_ref, w_ref, t_ref, keep_ref, pull, DAMPING if step else None)
        own = counted if final else plain
        g = [[g_ref[step, i, h] for h in range(planes)] for i in range(2)]
        acc, _ = run_substep(
            k, stages, acc_ref[...] if final else 0, (((begin - HALO) // SUBS, tiles, own),),
            own, plain, rows=(begin - k, rows_all - k), g=g,
        )
    store_part(part_out, acc)


def start_kernel(entries, *refs):
    (u_in, v_in, w_ref, f_ref, top, bottom, above, beneath, even, odd1, odd2, relay, part_ref,
     u_ref, v_ref, t_ref, part_out, keep_ref) = refs
    rows_all = u_ref.shape[1]
    tiles = (rows_all - 2 * HALO) // SUBS
    for halo, at in ((above, 0), (beneath, rows_all - HALO)):
        lay_halo(halo, at, ((0, u_ref, 2), (2, t_ref, 2), (4, v_ref, 2)))
    lay_edges(t_ref, top, bottom)
    copy_rows(HALO, rows_all - HALO, ((u_in, u_ref), (v_in, v_ref)))
    lay_targets(t_ref, f_ref, even, odd1, None, 0)
    lay_targets(t_ref, f_ref, even, odd2, relay, odd1.shape[1])
    pull = pull_of()
    damp0 = limited(part_ref, entries)
    plain, counted = (storer(u_ref, v_ref, False), storer(u_ref, v_ref, True))
    for step in range(SUBSTEPS):
        stages = Stages(u_ref, v_ref, w_ref, t_ref, keep_ref, pull, DAMPING if step else damp0)
        final = step == SUBSTEPS - 1
        own = counted if final else plain
        acc, _ = run_substep(
            1 + step, stages, jnp.zeros(TILE, jnp.float32) if final else 0, ((0, tiles, own),), plain, plain,
        )
    store_part(part_out, acc)


def sender(store, sends, f_ref, cuts, buffer, base, begin):
    def own(r, new_u, new_v, more):
        more = store(r, new_u, new_v, more)
        q = r - HALO
        row = base + q - begin * SUBS
        for i in range(2):
            for h in range(len(new_u[0])):
                f, u = (f_ref[i, q, h], new_u[i][h])
                store_sends(sends, buffer, row, sends[3].shape[1], u - cuts[0] * f, u - cuts[1] * f, i, h)
        return more

    return own


def finish_kernel(last, entries, *refs):
    if last:
        u_in, v_in, t_ref, w_ref, part_ref, u_out, v_out, keep_ref, u_ref, v_ref, u_flat, v_flat, u_nat, v_nat, sems = refs
    else:
        u_in, v_in, t_ref, w_ref, part_ref, f_ref, u_ref, v_ref, part_out, *sends, keep_ref = refs
    rows_all, planes = (u_ref.shape[1], u_ref.shape[2])
    tiles = (rows_all - 2 * HALO) // SUBS
    pull = pull_of()
    damp0 = limited(part_ref, entries)
    lines = planes * SUBS * SUBS

    def turn(tile):
        for p in range(SUBS):
            for h in range(planes):
                for i in range(2):
                    at = pl.ds(tile * SUBS * SUBS + p, SUBS, stride=SUBS)
                    out = pl.ds(pl.multiple_of(tile * lines + (p * planes + h) * SUBS, SUBS), SUBS)
                    u_nat[i, out, :] = u_flat[i * planes + h, at, :]
                    v_nat[i, out, :] = v_flat[i * planes + h, at, :] * (1.0 / STEP_SIZE)

    def send(begin, count):
        at = pl.ds(pl.multiple_of(begin * lines, lines), count * lines)
        for i, (nat, out) in enumerate(((u_nat, u_out), (v_nat, v_out))):
            for field in range(2):
                pltpu.make_async_copy(nat.at[field, at, :], out.at[field, at, :], sems.at[i]).start()

    def turn_and_send(tile):
        turn(jnp.maximum(tile - 1, 0))

        @pl.when(tile >= 2)
        def _():
            send(tile - 2, 1)

    for step in range(SUBSTEPS):
        k = 1 + SUBSTEPS + step
        source = (u_in, v_in) if step == 0 else (u_ref, v_ref)
        stages = Stages(*source, w_ref, t_ref, keep_ref, pull, damp0 if step == 0 else DAMPING)
        if step < SUBSTEPS - 1:
            plain = storer(u_ref, v_ref, False)
            run_substep(k, stages, 0, ((0, tiles, plain),), plain, plain)
        elif last:
            def own(r, new_u, new_v, more):
                for i in range(2):
                    for h in range(planes):
                        at = pl.ds(pl.multiple_of((r - HALO) * SUBS, SUBS), SUBS)
                        u_flat[i * planes + h, at, :] = new_u[i][h]
                        v_flat[i * planes + h, at, :] = new_v[i][h]
                return more

            run_substep(k, stages, 0, ((0, tiles, own),), own, own, turn_and_send)
        else:
            _, _, odd = section_flags()
            cuts = (jnp.full(TILE, odd, jnp.float32), jnp.full(TILE, 1.0 - odd, jnp.float32))
            store = storer(u_ref, v_ref, True)
            segments = [
                (begin, end, sender(store, sends, f_ref, cuts, buffer, base, begin))
                for begin, end, buffer, base in send_rows(tiles)
            ]
            more, _ = run_substep(k, stages, jnp.zeros(TILE, jnp.float32), segments, store, store)
    if not last:
        store_part(part_out, more)
        return

    for tile in range(tiles - 2, tiles):
        turn(tile)
    send(tiles - 3, 3)
    for i, (nat, out) in enumerate(((u_nat, u_out), (v_nat, v_out))):
        pltpu.make_async_copy(nat, out, sems.at[i]).wait()


def call(kernel, outs, operands, cost=0, scratch=(), copies=0):
    return pl.pallas_call(
        kernel,
        out_shape=tuple(jax.ShapeDtypeStruct(o, jnp.float32) for o in outs),
        in_specs=[VMEM] * len(operands),
        out_specs=tuple(pl.BlockSpec(memory_space=pl.ANY) if copies else VMEM for _ in outs),
        scratch_shapes=[pltpu.VMEM(shape, jnp.float32) for shape in scratch] + [pltpu.SemaphoreType.DMA((copies,))] * (copies > 0),
        cost_estimate=pl.CostEstimate(flops=cost, bytes_accessed=cost, transcendentals=0),
        compiler_params=pltpu.CompilerParams(vmem_limit_bytes=24 << 20),
    )(*operands)


def pairs(ones):
    return [p for a, b in ones for p in ((a, b), (b, a))]


def exchange(sends):
    n = lax.axis_size("sec")
    eb, ob, em, o1, o2 = sends
    even = pairs([(i, i + 1) for i in range(0, n - 1, 2)])
    odd = [(i, i + 1) for i in range(1, n - 1, 2)]
    far = [(i, j) for i, j in odd if i % 4 == 3]
    near = pairs([p for p in odd if p not in far])
    out = [(i, i + 4) for i, j in far] + [(j, j - 4) for i, j in far]
    back = [(i + 4, j) for i, j in far] + [(j - 4, i) for i, j in far]

    rob = lax.ppermute(ob, "sec", pairs(odd))
    away = lax.ppermute(o2, "sec", out)
    ro1 = lax.ppermute(o1, "sec", pairs(odd))
    ro2 = lax.ppermute(o2, "sec", near)
    reb = lax.ppermute(eb, "sec", even)
    rem = lax.ppermute(em, "sec", even)
    relay = lax.ppermute(away, "sec", back)
    return reb, rob, rem, ro1, ro2, relay


def viewed(x):
    fields, rows, columns = x.shape
    x = x.reshape(fields, rows // SUBS, SUBS, columns // LANES, LANES).transpose(0, 1, 3, 2, 4)
    return x.reshape(fields, rows * columns // LANES, LANES)


def unviewed(x, rows, columns):
    x = x.reshape(x.shape[0], rows // SUBS, columns // LANES, SUBS, LANES).transpose(0, 1, 3, 2, 4)
    return x.reshape(x.shape[0], rows, columns)


def on_device(start_offsets, section_flow, fixed_nodes, links_across, links_down):
    axes = ("sec", "strip")
    sections, strips = (lax.axis_size("sec"), lax.axis_size("strip"))
    devices = sections * strips
    _, rows, columns = fixed_nodes.shape
    entries = 2.0 * sections * strips * rows * columns
    planes = columns // (SUBS * LANES)
    tiles = rows // SUBS
    wide = lambda fields, count: (fields, count, planes) + TILE
    half = (tiles - 2) // 2 * SUBS
    main = rows - 2 * SUBS
    send_shapes = [wide(2, 2 * SUBS), wide(2, 2 * SUBS), wide(2, main), wide(2, half), wide(2, main - half)]
    rows_all = rows + 2 * HALO
    full, keep, part_shape = (wide(2, rows_all), wide(4, rows_all), (devices, 1, LANES))
    up = [(i, i + 1) for i in range(strips - 1)]
    dn = [(j, i) for i, j in up]
    natural = rows * columns // LANES
    u, f, *sends = call(
        prepare_kernel, [full, wide(2, rows)] + send_shapes,
        [viewed(start_offsets[:, 0]), viewed(section_flow[:, 0])], cost=4 << 20,
    )
    (w,) = call(
        weights_kernel, [wide(3, rows_all)],
        [viewed(x)[0] for x in (fixed_nodes, links_across, links_down)], cost=4 << 20,
    )
    v, part = (None, None)
    for sweep in range(SWEEPS):
        first, last = (sweep == 0, sweep == SWEEPS - 1)
        if not first:
            part = lax.all_to_all(part, axes, 0, 0)
        reb, rob, rem, ro1, ro2, relay = exchange(sends)
        fields = 7 if first else 6
        top, bottom = call(
            functools.partial(edge_kernel, first), [wide(fields, SUBS)] * 2, [reb, rob, f, u, w if first else v], cost=1 << 18,
        )
        above = lax.ppermute(bottom, "strip", up)
        beneath = lax.ppermute(top, "strip", dn)
        received = [f, top, bottom, above, beneath, rem, ro1]
        if first:
            u, w, t, v, g, acc = call(
                early_kernel, [full, wide(3, rows_all), full, full, (SUBSTEPS, 2, planes) + TILE, TILE],
                [u, w] + received, cost=8 << 20, scratch=[keep],
            )
            u, t, v, part = call(
                late_kernel, [full, full, full, part_shape], [u, w, t, v, g, acc, f, rem, ro2, relay],
                cost=8 << 20, scratch=[keep],
            )
        else:
            u, v, t, part = call(
                functools.partial(start_kernel, entries), [full, full, full, part_shape],
                [u, v, w] + received + [ro2, relay, part], cost=16 << 20, scratch=[keep],
            )
        part = lax.all_to_all(part, axes, 0, 0)
        if last:
            u, v = call(
                functools.partial(finish_kernel, True, entries), [(2, natural, LANES)] * 2,
                [u, v, t, w, part], cost=16 << 20, scratch=[keep, full, full] + [(2 * planes, rows * SUBS, LANES)] * 2 + [(2, natural, LANES)] * 2, copies=2,
            )
        else:
            u, v, part, *sends = call(
                functools.partial(finish_kernel, False, entries), [full, full, part_shape] + send_shapes,
                [u, v, t, w, part, f], cost=16 << 20, scratch=[keep],
            )
    return (unviewed(u, rows, columns)[:, None], unviewed(v, rows, columns)[:, None])


def solution(mesh):
    return jax.shard_map(
        on_device,
        mesh=mesh,
        in_specs=(
            P(None, "sec", "strip", None),
            P(None, "sec", "strip", None),
            P("sec", "strip", None),
            P("sec", "strip", None),
            P("sec", "strip", None),
        ),
        out_specs=(P(None, "sec", "strip", None), P(None, "sec", "strip", None)),
        check_vma=False,
    )
```
